512 devices in a mesh: group: 4 (over z_lo), tile: 128 (over x, z_hi, y, core).
Axes of the slice: x: 4, y: 4, z: 16 (z_hi: 4, z_lo: 4; z = z_hi * 4 + z_lo), core: 2. Of those that a mesh axis runs over, the one named last changes fastest.
Arguments:
- potential: float32 [64, 131072], P('group', 'tile'), may hold values from -6 to 6
- species_inputs: bfloat16 [7, 64, 131072], P(None, 'group', 'tile'), may hold values from -6 to 6
- diffusion: float32 [4, 131072], P(None, 'tile'), may hold values from 0.02 to 0.2
- neighbours: int32 [4, 131072], P(None, 'tile'), may hold values from 0 to 1535, as said below
- sunlit_column_index: int32 [4, 128, 256], P('group', 'tile'), may hold values from 0 to 255, each once within a row
- day_count: int32 [4, 128], P('group', 'tile'), may hold values from 0 to 256, as said below
- zenith: bfloat16 [4, 128, 256], P('group', 'tile'), may hold values from 0.099609375 to 1
- lw_first: bfloat16 [8, 64], replicated, may hold values from -2 to 2
- lw_bias: float32 [64], replicated, may hold values from -3 to 3
- lw_second: bfloat16 [64, 64], replicated, may hold values from -0.75 to 0.75
- lw_depth: bfloat16 [64, 256], replicated, may hold values from -0.75 to 0.75
- lw_fraction: bfloat16 [64, 256], replicated, may hold values from -0.75 to 0.75
- sw_first: bfloat16 [8, 64], replicated, may hold values from -2 to 2
- sw_bias: float32 [64], replicated, may hold values from -3 to 3
- sw_second: bfloat16 [64, 64], replicated, may hold values from -0.75 to 0.75
- sw_depth: bfloat16 [64, 224], replicated, may hold values from -0.75 to 0.75
- solar_flux: float32 [224], replicated, may hold values from 0.5 to 2
Outputs:
- evolved: float32 [64, 131072], P('group', 'tile')
The draws below stay inside these ranges and needn't reach their ends.
Inputs may be any that keep to these rules, and one draw needn't show every extreme that they name: neighbours[k, c] - 256 - (c mod 1024) is a nonzero offset between -256 and 256. `sunlit_column_index`: each list [g, t, :] is a permutation of 0 .. 255. day_count[g, 2 i] + day_count[g, 2 i + 1] = 256 for every g and i.
All inputs are finite; a program needn't handle non-finite values.
Results may differ from the reference program's by a relative error of at most 0.0003.
Values may be sent and summed in bfloat16 or wider, within the bound.
A program may use at most 128 MiB of HBM per device.

```python
import math
from functools import partial
import jax
import jax.numpy as jnp
from jax import lax

LEV = 64
COL_DEV = 256
GAS = 7
HID = 64
GPT = 256
SWG = 224
NB = 4
HW = 256
FIN = 8
TILE_COLS = 1024
NCOL = 131072
N_GROUP = 4
N_TILE = 128


def draw_neighbours(key, part):
    reaches = jax.random.randint(jax.random.fold_in(key, 101), (NB, NCOL), 1, HW + 1)
    sign_of = jax.random.randint(jax.random.fold_in(key, 102), (NB, NCOL), 0, 2) * 2 - 1
    column = jnp.arange(NCOL, dtype=jnp.int32)
    within = column % TILE_COLS
    offset_all = reaches * sign_of
    opening_line = jnp.arange(NB, dtype=jnp.int32)[:, None] == 0
    offset_all = jnp.where(opening_line & (within[None, :] == 0), -HW, offset_all)
    offset_all = jnp.where(opening_line & (within[None, :] == TILE_COLS - 1), HW, offset_all)
    return (within[None, :] + HW + offset_all).astype(jnp.int32)


def draw_day_count(key, part):
    evens = jax.random.randint(jax.random.fold_in(key, 201), (N_GROUP, N_TILE // 2), 0, COL_DEV + 1)
    chosen = jax.random.randint(jax.random.fold_in(key, 202), (N_GROUP, 1), 0, N_TILE // 2)
    extreme = jax.random.randint(jax.random.fold_in(key, 203), (N_GROUP, 1), 0, 2) * COL_DEV
    pair_ids = jnp.arange(N_TILE // 2, dtype=jnp.int32)[None, :]
    evens = jnp.where(pair_ids == chosen, extreme, evens)
    odds = COL_DEV - evens
    return jnp.stack([evens, odds], axis=2).reshape(N_GROUP, N_TILE).astype(jnp.int32)


def level_of(stream_key, dims, cuts, least, high):
    loudness = 1.0
    for axis_at, shards_of in cuts:
        heights = jax.random.uniform(jax.random.fold_in(jax.random.fold_in(stream_key, 6), axis_at), (shards_of,), jnp.float32, least / len(cuts), high / len(cuts))
        loudness = loudness * jnp.repeat(jnp.exp(heights), dims[axis_at] // shards_of).reshape((-1,) + (1,) * (len(dims) - 1 - axis_at))
    return loudness


def gaussian(key, extent, width, reach, shards=(), held_as=jnp.bfloat16):
    drawn = width * jax.random.normal(key, extent, jnp.float32)
    if shards:
        drawn = drawn * level_of(key, extent, shards, -0.22, 0.18)
    return jnp.clip(drawn, -reach, reach).astype(held_as)


def setup_inputs(seed: int = 0) -> dict:
    streams_of = jax.random.split(jax.random.key(seed), 18)
    potential = gaussian(streams_of[0], (LEV, NCOL), 1.0, 6.0, ((0, 4), (1, 128)), jnp.float32)
    species_inputs = gaussian(streams_of[1], (GAS, LEV, NCOL), 1.0, 6.0, ((1, 4), (2, 128)))
    diffusion = jnp.clip(jnp.exp(math.log(0.2) - 2.3025851 * jax.random.uniform(streams_of[2], (NB, NCOL), jnp.float32) ** level_of(streams_of[2], (NB, NCOL), ((1, 128),), -0.2, 0.2)), 0.02, 0.2)
    neighbours = draw_neighbours(jax.random.fold_in(streams_of[17], 71), 0)
    sunlit_column_index = jax.vmap(lambda own: jax.random.permutation(own, COL_DEV))(jax.random.split(streams_of[4], N_GROUP * N_TILE)).reshape((N_GROUP, N_TILE, COL_DEV)).astype(jnp.int32)
    day_count = draw_day_count(jax.random.fold_in(streams_of[17], 71), 0)
    zenith = jnp.clip(0.099609375 + 0.9003906 * jax.random.uniform(streams_of[6], (N_GROUP, N_TILE, COL_DEV), jnp.float32) ** level_of(streams_of[6], (N_GROUP, N_TILE, COL_DEV), ((0, 4), (1, 128)), -0.2, 0.2), 0.099609375, 1.0).astype(jnp.bfloat16)
    lw_first = gaussian(streams_of[7], (FIN, HID), FIN ** -0.5, 2.0)
    lw_bias = gaussian(streams_of[8], (HID,), 0.5, 3.0, (), jnp.float32)
    lw_second = gaussian(streams_of[9], (HID, HID), HID ** -0.5, 0.75)
    lw_depth = gaussian(streams_of[10], (HID, GPT), HID ** -0.5, 0.75)
    lw_fraction = gaussian(streams_of[11], (HID, GPT), HID ** -0.5, 0.75)
    sw_first = gaussian(streams_of[12], (FIN, HID), FIN ** -0.5, 2.0)
    sw_bias = gaussian(streams_of[13], (HID,), 0.5, 3.0, (), jnp.float32)
    sw_second = gaussian(streams_of[14], (HID, HID), HID ** -0.5, 0.75)
    sw_depth = gaussian(streams_of[15], (HID, SWG), HID ** -0.5, 0.75)
    solar_flux = jnp.clip(jnp.exp(jax.random.uniform(streams_of[16], (SWG,), jnp.float32, math.log(0.5), math.log(2.0))), 0.5, 2.0)
    return {"potential": potential, "species_inputs": species_inputs, "diffusion": diffusion, "neighbours": neighbours, "sunlit_column_index": sunlit_column_index, "day_count": day_count, "zenith": zenith, "lw_first": lw_first, "lw_bias": lw_bias, "lw_second": lw_second, "lw_depth": lw_depth, "lw_fraction": lw_fraction, "sw_first": sw_first, "sw_bias": sw_bias, "sw_second": sw_second, "sw_depth": sw_depth, "solar_flux": solar_flux}


depth_scale = 0.1
heat_scale = 12.0


def tendency(field, neighbours, diffusion):
    tile_cols = COL_DEV * N_GROUP
    grand_profile_tally = tile_cols * N_TILE
    column = jnp.arange(grand_profile_tally, dtype=jnp.int32)
    anchor = column - column % tile_cols
    outcome_state = jnp.zeros_like(field)
    for branch in range(NB):
        target = ((anchor + neighbours[branch] - HW) % grand_profile_tally).astype(jnp.int32)
        outcome_state = outcome_state + diffusion[branch] * (field[:, target] - field)
    return outcome_state


def hidden_layers(inputs, w_first, bias, w_second):
    flat_in = inputs.reshape(inputs.shape[0], -1)
    layer_one = jax.nn.silu(jnp.dot(w_first.T, flat_in, preferred_element_type=jnp.float32) + bias[:, None]).astype(jnp.bfloat16)
    return jax.nn.silu(jnp.dot(w_second.T, layer_one, preferred_element_type=jnp.float32)).astype(jnp.bfloat16)


def longwave(inputs, weights):
    w_first, bias, w_second, w_depth, w_fraction = weights
    vertical_levels, col_count = inputs.shape[1], inputs.shape[2]
    hidden = hidden_layers(inputs, w_first, bias, w_second)
    depth = depth_scale * jax.nn.softplus(jnp.dot(w_depth.T, hidden, preferred_element_type=jnp.float32)).reshape(-1, vertical_levels, col_count)
    fraction = jax.nn.softplus(jnp.dot(w_fraction.T, hidden, preferred_element_type=jnp.float32)).reshape(-1, vertical_levels, col_count)
    above = jnp.cumsum(depth, axis=1) - depth
    planck = jnp.exp(0.25 * inputs[0].astype(jnp.float32))
    emitted = jnp.sum(fraction * (1.0 - jnp.exp(-depth)) * jnp.exp(-above), axis=0)
    return -(heat_scale / depth.shape[0]) * planck * emitted


def shortwave(inputs, cosine, weights):
    w_first, bias, w_second, w_depth, solar_flux = weights
    vertical_levels, col_count = inputs.shape[1], inputs.shape[2]
    hidden = hidden_layers(inputs, w_first, bias, w_second)
    depth = depth_scale * jax.nn.softplus(jnp.dot(w_depth.T, hidden, preferred_element_type=jnp.float32)).reshape(-1, vertical_levels, col_count)
    above = jnp.cumsum(depth, axis=1) - depth
    slant = 1.0 / cosine
    beam = solar_flux[:, None, None] * cosine * jnp.exp(-above * slant) * (1.0 - jnp.exp(-depth * slant))
    return (heat_scale / depth.shape[0]) * jnp.sum(beam, axis=0)


def blockwise(kernel, inputs, cosine, weights):
    span_cols = inputs.shape[2]
    block_cols = 128 if span_cols % 128 == 0 else span_cols

    def one_block(begin_at):
        part_in = lax.dynamic_slice_in_dim(inputs, begin_at, block_cols, 2)
        if cosine is None:
            return kernel(part_in, weights)
        return kernel(part_in, lax.dynamic_slice_in_dim(cosine, begin_at, block_cols, 0), weights)

    starts = jnp.arange(span_cols // block_cols, dtype=jnp.int32) * block_cols
    stacked = lax.map(one_block, starts)
    return jnp.transpose(stacked, (1, 0, 2)).reshape(stacked.shape[1], span_cols)


def reference(potential, species_inputs, diffusion, neighbours, sunlit_column_index, day_count, zenith, lw_first, lw_bias, lw_second, lw_depth, lw_fraction, sw_first, sw_bias, sw_second, sw_depth, solar_flux):
    update = partial(tendency, neighbours=neighbours, diffusion=diffusion)
    first = potential + update(potential)
    second = 0.75 * potential + 0.25 * (first + update(first))
    tertile_portion = potential / 3.0 + (2.0 / 3.0) * (second + update(second))
    features = jnp.concatenate([tertile_portion.astype(jnp.bfloat16)[None], species_inputs], axis=0)
    layout = features.reshape(GAS + 1, LEV, N_TILE, N_GROUP, COL_DEV)
    slots = jnp.arange(COL_DEV, dtype=jnp.int32)
    long_weights = (lw_first, lw_bias, lw_second, lw_depth, lw_fraction)
    short_weights = (sw_first, sw_bias, sw_second, sw_depth, solar_flux)

    def portion_each_processor(number):
        tile_no = number // N_GROUP
        group_no = number % N_GROUP
        block = lax.dynamic_index_in_dim(layout, tile_no, 2, keepdims=False)
        block = lax.dynamic_index_in_dim(block, group_no, 2, keepdims=False)
        cosine = zenith[group_no, tile_no].astype(jnp.float32)
        listed = (sunlit_column_index[group_no, tile_no][:, None] == slots[None, :]) & (slots[:, None] < day_count[group_no, tile_no])
        daylit = jnp.sum(listed.astype(jnp.float32), axis=0)
        longwave_heating_rate = blockwise(longwave, block, None, long_weights)
        short_heat = blockwise(shortwave, block, cosine, short_weights)
        return longwave_heating_rate + short_heat * daylit

    heats = lax.map(portion_each_processor, jnp.arange(N_TILE * N_GROUP, dtype=jnp.int32))
    heating = jnp.transpose(heats.reshape(N_TILE, N_GROUP, LEV, COL_DEV), (2, 0, 1, 3)).reshape(LEV, -1)
    return tertile_portion + update(tertile_portion) + heating
```

```python
import functools
import math

import jax
import jax.numpy as jnp
from jax import lax
from jax.experimental import pallas as pl
from jax.experimental.pallas import tpu as pltpu
from jax.sharding import PartitionSpec as P

COL_DEV = 256
HALF = 128
TILE = 1024
NB = 4
HW = 256
GAS = 7
f32, bf16 = jnp.float32, jnp.bfloat16
MESH = pl.DeviceIdType.MESH
LOG2E = 1.4426950408889634
CLAMP = 120.0

def silu(x):
    return 0.5 * x * (1.0 + jnp.tanh(0.5 * x))

def soft2(y):
    return jnp.maximum(y, jnp.log2(1.0 + jnp.exp2(jnp.minimum(y, CLAMP))))

def hi_lo(w):
    hi = w.astype(bf16)
    return hi, (w - hi.astype(f32)).astype(bf16)

def prep_first(w_first):
    wt = jnp.transpose(w_first.astype(f32))
    col = lax.broadcasted_iota(jnp.int32, (8, 128), 1)
    row = lax.broadcasted_iota(jnp.int32, (8, 128), 0)
    spread = (col // 16 == row).astype(f32)
    wide = jnp.dot(wt.astype(bf16), spread.astype(bf16), preferred_element_type=f32)
    return wide

def rad_kernel(cols_ref, work_ref, mu_ref, lw1_ref, lb_ref, lw2_ref, ld_ref, lf_ref, sw1_ref, sb_ref, sw2_ref, sd_ref, flux_ref,
               lw_out, sw_out, a1, b1, a2, b2, ah, bh, h1, h2, s_ref, e_ref, ss_ref, *, which):
    def first_into(dst, w_ref):
        wide = prep_first(w_ref[...])
        lane = lax.broadcasted_iota(jnp.int32, (64, 128), 1) % 16
        for l in range(16):
            dst[l * 64:(l + 1) * 64, :] = jnp.where(lane == l, wide, 0.0).astype(bf16)
    def second_into(dst, w_ref):
        wt = jnp.transpose(w_ref[...].astype(f32))
        z = jnp.zeros((64, 64), f32)
        for i in range(2):
            dst[i*64:(i+1)*64, :] = jnp.concatenate([wt if j == i else z for j in range(2)], axis=1).astype(bf16)
    first_into(a1, lw1_ref); first_into(b1, sw1_ref)
    second_into(a2, lw2_ref); second_into(b2, sw2_ref)
    d = jnp.transpose(ld_ref[...].astype(f32)) * LOG2E
    f = jnp.transpose(lf_ref[...].astype(f32)) * LOG2E
    inter = jnp.concatenate([d.reshape(32, 8, 64), f.reshape(32, 8, 64)], axis=1).reshape(512, 64)
    hi, lo = hi_lo(inter)
    ah[...] = jnp.concatenate([hi, lo], axis=1)
    sd = jnp.transpose(sd_ref[...].astype(f32)) * LOG2E
    hi, lo = hi_lo(sd)
    bh[...] = jnp.concatenate([hi, lo], axis=1)

    bl = jnp.transpose(jnp.broadcast_to(lb_ref[...], (128, 64)))
    bs = jnp.transpose(jnp.broadcast_to(sb_ref[...], (128, 64)))
    lbias = jnp.concatenate([bl, bl], axis=1)

    def hidden(x_ref, first, second, bias, width, blk):
        x = x_ref[:, pl.ds(pl.multiple_of(blk * 16, 16), 16), :].reshape(128, width)
        for q in range(8):
            pre = jnp.dot(first[q*128:(q+1)*128, :], x, preferred_element_type=f32)
            pre = pre.reshape(2, 64, width) + bias[None]
            one = silu(pre).reshape(128, width).astype(bf16)
            two = silu(jnp.dot(second[...], one, preferred_element_type=f32))
            h2[q*128:(q+1)*128, :width] = two.astype(bf16)

    if "l" in which:
        s_ref[...] = jnp.zeros_like(s_ref)
        e_ref[...] = jnp.ones_like(e_ref)
        @pl.loop(0, 4)
        def _(blk):
            hidden(cols_ref, a1, a2, lbias, 256, blk)
            @pl.loop(0, 16)
            def _(l):
                h = h2[pl.ds(pl.multiple_of(l * 64, 64), 64), :]
                hh = jnp.concatenate([h, h], axis=0)
                y = jnp.dot(ah[...], hh, preferred_element_type=f32)
                acc = jnp.zeros((8, 256), f32)
                for g in range(32):
                    tau = soft2(y[g*16:g*16+8])
                    frac = soft2(y[g*16+8:g*16+16])
                    s = s_ref[g*8:g*8+8] + tau
                    s_ref[g*8:g*8+8] = s
                    e = jnp.exp2(-0.1 * s)
                    acc = acc + frac * (e_ref[g*8:g*8+8] - e)
                    e_ref[g*8:g*8+8] = e
                lw_out[pl.ds(blk*16 + l, 1), :] = jnp.sum(acc, axis=0, keepdims=True)
        t = cols_ref[0].astype(f32)
        lw_out[...] = lw_out[...] * (-(12.0 / 256) * math.log(2.0)) * jnp.exp(0.25 * t)
    else:
        lw_out[...] = jnp.zeros_like(lw_out)
    if "s" in which:
        mu = mu_ref[...]
        slope = jnp.broadcast_to(-0.1 / mu, (8, 128))
        muf = jnp.broadcast_to(10.0 * mu, (224, 128))
        lf2 = jnp.transpose(jnp.broadcast_to(jnp.log2(flux_ref[...]), (128, 224)))
        ss_ref[...] = -muf * lf2
        g0 = jnp.sum(jnp.exp2(lf2), axis=0, keepdims=True)
        carry0 = g0
        def blk_body(blk, prev):
            hidden(work_ref, b1, b2, bs, 128, blk)
            def lev(lp, prev):
                r = pl.multiple_of(lp * 128, 128)
                h = jnp.concatenate([h2[pl.ds(r, 64), :128], h2[pl.ds(r + 64, 64), :128]], axis=1)
                hh = jnp.concatenate([h, h], axis=0)
                y = jnp.dot(bh[...], hh, preferred_element_type=f32)
                acc0 = jnp.zeros((8, 128), f32)
                acc1 = jnp.zeros((8, 128), f32)
                for g in range(28):
                    s = ss_ref[g*8:g*8+8]
                    s = s + soft2(y[g*8:g*8+8, :128])
                    acc0 = acc0 + jnp.exp2(s * slope)
                    s = s + soft2(y[g*8:g*8+8, 128:])
                    ss_ref[g*8:g*8+8] = s
                    acc1 = acc1 + jnp.exp2(s * slope)
                c0 = jnp.sum(acc0, axis=0, keepdims=True)
                c1 = jnp.sum(acc1, axis=0, keepdims=True)
                sw_out[pl.ds(blk*16 + lp*2, 1), :] = prev - c0
                sw_out[pl.ds(blk*16 + lp*2 + 1, 1), :] = c0 - c1
                return c1
            return lax.fori_loop(0, 8, lev, prev)
        lax.fori_loop(0, 4, blk_body, carry0)
        sw_out[...] = sw_out[...] * mu * (12.0 / 224)
    else:
        sw_out[...] = jnp.zeros_like(sw_out)

def radiate(cols, work, mu, lw, sw, which="ls"):
    lw1, lb, lw2, ld, lf = lw
    sw1, sb, sw2, sd, fl = sw
    return pl.pallas_call(
        functools.partial(rad_kernel, which=which),
        out_shape=(jax.ShapeDtypeStruct((64, 256), f32), jax.ShapeDtypeStruct((64, 128), f32)),
        in_specs=[pl.BlockSpec(memory_space=pltpu.VMEM)] * 13,
        out_specs=[pl.BlockSpec(memory_space=pltpu.VMEM)] * 2,
        scratch_shapes=[pltpu.VMEM((1024, 128), bf16), pltpu.VMEM((1024, 128), bf16), pltpu.VMEM((128, 128), bf16), pltpu.VMEM((128, 128), bf16),
                        pltpu.VMEM((512, 128), bf16), pltpu.VMEM((224, 128), bf16), pltpu.VMEM((1024, 256), bf16), pltpu.VMEM((1024, 256), bf16),
                        pltpu.VMEM((256, 256), f32), pltpu.VMEM((256, 256), f32), pltpu.VMEM((224, 128), f32)],
        compiler_params=pltpu.CompilerParams(vmem_limit_bytes=50 * 2**20), name="rad_" + which,
    )(cols, work, mu, lw1, lb.reshape(1, 64), lw2, ld, lf, sw1, sb.reshape(1, 64), sw2, sd, fl.reshape(1, 224))


N_GROUP = 4
WIDE = TILE + 6 * HW
TABLE = TILE + 4 * HW


def section(src, tables, weights, src_shift, lo, hi, put):
    @pl.loop(lo, hi)
    def _(b):
        at = lambda j: pl.ds(pl.multiple_of(j * 128, 128), 128)
        reach = [src[:, at(b - src_shift - 2 + s)] for s in range(5)]
        mid = reach[2]
        home = lax.rem(b + 2, 8) * 128
        total = jnp.zeros_like(mid)
        for k in range(NB):
            rel = jnp.broadcast_to(tables[k : k + 1, at(b - 2)] - home, mid.shape)
            lane = jnp.bitwise_and(rel, 127)
            which = jnp.right_shift(rel, 7)
            near = taken(reach[0], lane)
            for s in range(1, 5):
                near = jnp.where(which == s, taken(reach[s], lane), near)
            total = total + weights[k : k + 1, at(b - 2)] * (near - mid)
        put(b, at, mid, total)


def taken(rows, lane):
    parts = [
        jnp.take_along_axis(rows[i : i + 8], lane[i : i + 8], axis=1, mode="promise_in_bounds")
        for i in range(0, rows.shape[0], 8)
    ]
    return jnp.concatenate(parts, axis=0)


def greet(group_peers, tile_peers):
    barrier = pltpu.get_barrier_semaphore()
    for p in group_peers:
        pl.semaphore_signal(barrier, inc=1, device_id={"group": p}, device_id_type=MESH)
    for p in tile_peers:
        pl.semaphore_signal(barrier, inc=1, device_id={"tile": p}, device_id_type=MESH)
    pl.semaphore_wait(barrier, len(group_peers) + len(tile_peers))


def slots_of(listing):
    cols = lax.broadcasted_iota(jnp.int32, (COL_DEV, COL_DEV), 0)
    slot = lax.broadcasted_iota(jnp.int32, (COL_DEV, COL_DEV), 1).astype(f32)
    return jnp.sum(jnp.where(listing == cols, slot, 0.0), axis=1, keepdims=True)


def gather_kernel(
    pot, species, diff, nbr, listing_ref, count_ref, zen_ref,
    base_out, cols, work, mu_out,
    fe, f1, f2, te, third16, tables, weights, outgoing, arriving, mu_send, mu_arrive,
    local, h_send, h_recv, g_send, g_recv, t_send, t_recv, e_send, e_recv, d_send, d_recv,
):
    me, tile = lax.axis_index("group"), lax.axis_index("tile")
    n_tile = lax.axis_size("tile")
    right, left = lax.rem(tile + 1, n_tile), lax.rem(tile + n_tile - 1, n_tile)
    partner = tile + 1 - 2 * lax.rem(tile, 2)
    peers = [lax.rem(me + d, N_GROUP) for d in range(1, N_GROUP)]

    def remote(src, dst, send, recv, where):
        return pltpu.make_async_remote_copy(
            src_ref=src, dst_ref=dst, send_sem=send, recv_sem=recv,
            device_id=where, device_id_type=MESH)

    own = [
        pltpu.make_async_copy(pot, fe.at[:, 3 * HW : 3 * HW + TILE], local.at[0]),
        pltpu.make_async_copy(diff, weights.at[:, 2 * HW : 2 * HW + TILE], local.at[1]),
        pltpu.make_async_copy(nbr, tables.at[:, 2 * HW : 2 * HW + TILE], local.at[2]),
    ]
    levels = pl.ds(pl.multiple_of(me * 16, 16), 16)
    columns_of = lambda g: pl.ds(pl.multiple_of(g * COL_DEV, COL_DEV), COL_DEV)
    own_gas = pltpu.make_async_copy(
        species.at[:, :, columns_of(me)], cols.at[1 : GAS + 1, levels, :], local.at[3])
    for c in own:
        c.start()
    own_gas.start()
    greet(peers, (left, right))
    halo = [
        remote(pot.at[:, : 3 * HW], fe.at[:, 3 * HW + TILE :], h_send.at[0], h_recv.at[0], {"tile": left}),
        remote(pot.at[:, TILE - 3 * HW :], fe.at[:, : 3 * HW], h_send.at[1], h_recv.at[1], {"tile": right}),
        remote(diff.at[:, : 2 * HW], weights.at[:, 2 * HW + TILE :], h_send.at[2], h_recv.at[2], {"tile": left}),
        remote(diff.at[:, TILE - 2 * HW :], weights.at[:, : 2 * HW], h_send.at[3], h_recv.at[3], {"tile": right}),
        remote(nbr.at[:, : 2 * HW], tables.at[:, 2 * HW + TILE :], h_send.at[4], h_recv.at[4], {"tile": left}),
        remote(nbr.at[:, TILE - 2 * HW :], tables.at[:, : 2 * HW], h_send.at[5], h_recv.at[5], {"tile": right}),
    ]
    for c in halo:
        c.start()
    gas = [
        remote(species.at[:, :, columns_of(p)], cols.at[1 : GAS + 1, levels, :],
               g_send.at[i], g_recv.at[i], {"group": p})
        for i, p in enumerate(peers)
    ]
    for c in gas:
        c.start()
    for c in own:
        c.wait()
    for c in halo:
        c.wait()

    def put_first(b, at, mid, total):
        f1[:, at(b)] = mid + total

    def put_second(b, at, mid, total):
        f2[:, at(b)] = 0.75 * fe[:, at(b)] + 0.25 * (mid + total)

    def put_third(b, at, mid, total):
        value = fe[:, at(b)] / 3.0 + (2.0 / 3.0) * (mid + total)
        te[:, at(b - 4)] = value
        third16[:, at(b - 6)] = value.astype(bf16)

    section(fe, tables, weights, 0, 2, 18, put_first)
    section(f1, tables, weights, 0, 4, 16, put_second)
    section(f2, tables, weights, 0, 6, 14, put_third)

    warm = [
        remote(third16.at[:, columns_of(p)], cols.at[0, levels, :],
               t_send.at[i], t_recv.at[i], {"group": p})
        for i, p in enumerate(peers)
    ]
    for c in warm:
        c.start()
    edges = [
        remote(te.at[:, HW : 2 * HW], te.at[:, HW + TILE :], e_send.at[0], e_recv.at[0], {"tile": left}),
        remote(te.at[:, TILE : HW + TILE], te.at[:, :HW], e_send.at[1], e_recv.at[1], {"tile": right}),
    ]
    for c in edges:
        c.start()
    cols[0, levels, :] = third16[:, columns_of(me)]

    count = count_ref[...].astype(f32)
    slot = slots_of(listing_ref[...])
    place = lax.broadcasted_iota(jnp.int32, (COL_DEV, HALF), 1).astype(f32)
    kept = (slot == place) & (place < count)
    sent = (slot == place + count - HALF) & (place >= COL_DEV - count)
    pick = jnp.concatenate([kept.astype(f32), sent.astype(f32)], axis=1).astype(bf16)

    own_gas.wait()
    for c in gas:
        c.wait()
    for c in warm:
        c.wait()
    picked = jnp.dot(cols[...].reshape((GAS + 1) * 64, COL_DEV), pick, preferred_element_type=f32)
    outgoing[...] = picked[:, HALF:].astype(bf16).reshape(GAS + 1, 64, HALF)
    mu_picked = jnp.dot(jnp.broadcast_to(zen_ref[...], (16, COL_DEV)), pick, preferred_element_type=f32)
    mu_send[...] = mu_picked[:8, HALF:]
    swap = [
        remote(outgoing, arriving, d_send.at[0], d_recv.at[0], {"tile": partner}),
        remote(mu_send, mu_arrive, d_send.at[1], d_recv.at[1], {"tile": partner}),
    ]
    for c in swap:
        c.start()
    for c in edges:
        c.wait()

    def put_base(b, at, mid, total):
        base_out[:, at(b - 6)] = mid + total

    section(te, tables, weights, 4, 6, 14, put_base)
    for c in swap:
        c.wait()
    kept_cols = picked[:, :HALF].astype(bf16).reshape(GAS + 1, 64, HALF)
    work[...] = kept_cols + arriving[...]
    mu_out[...] = mu_picked[:1, :HALF] + mu_arrive[:1, :]


def spread_kernel(
    lw, sw, base, listing_ref, count_ref, out,
    ret, heat, slab, d_send, d_recv, s_send, s_recv,
):
    me, tile = lax.axis_index("group"), lax.axis_index("tile")
    partner = tile + 1 - 2 * lax.rem(tile, 2)
    peers = [lax.rem(me + d, N_GROUP) for d in range(1, N_GROUP)]

    def remote(src, dst, send, recv, where):
        return pltpu.make_async_remote_copy(
            src_ref=src, dst_ref=dst, send_sem=send, recv_sem=recv,
            device_id=where, device_id_type=MESH)

    greet(peers, (partner,))
    back = remote(sw, ret, d_send, d_recv, {"tile": partner})
    back.start()
    count = count_ref[...].astype(f32)
    slot = slots_of(listing_ref[...])
    diag = lax.broadcasted_iota(jnp.int32, (COL_DEV, COL_DEV), 0) == lax.broadcasted_iota(
        jnp.int32, (COL_DEV, COL_DEV), 1)
    slot = jnp.sum(jnp.where(diag, slot, 0.0), axis=0, keepdims=True)
    here = slot < jnp.minimum(count, HALF)
    there = (slot >= HALF) & (slot < count)
    index = jnp.where(there, slot + HALF - count, slot).astype(jnp.int32)
    index = jnp.bitwise_and(index, HALF - 1)
    here, there = here.astype(f32), there.astype(f32)
    back.wait()
    for half in range(2):
        part = slice(half * HALF, half * HALF + HALF)
        lane = jnp.broadcast_to(index[:, part], (64, HALF))
        heat[:, part] = (
            lw[:, part]
            + here[:, part] * taken(sw[...], lane)
            + there[:, part] * taken(ret[...], lane)
        )
    levels_of = lambda g: pl.ds(pl.multiple_of(g * 16, 16), 16)
    columns = pl.ds(pl.multiple_of(me * COL_DEV, COL_DEV), COL_DEV)
    sends = [
        remote(heat.at[levels_of(p), :], slab.at[:, columns], s_send.at[i], s_recv.at[i], {"group": p})
        for i, p in enumerate(peers)
    ]
    for c in sends:
        c.start()
    slab[:, columns] = heat[levels_of(me), :]
    for c in sends:
        c.wait()
    out[...] = base[...] + slab[...]


VMEM = pl.BlockSpec(memory_space=pltpu.VMEM)
ANY = pl.BlockSpec(memory_space=pl.ANY)


def per_device(
    potential, species_inputs, diffusion, neighbours, sunlit_column_index, day_count, zenith,
    lw_first, lw_bias, lw_second, lw_depth, lw_fraction,
    sw_first, sw_bias, sw_second, sw_depth, solar_flux,
):
    listing = sunlit_column_index.reshape(1, COL_DEV)
    dma = pltpu.SemaphoreType.DMA
    base, cols, work, mu = pl.pallas_call(
        gather_kernel,
        out_shape=(
            jax.ShapeDtypeStruct((16, TILE), f32),
            jax.ShapeDtypeStruct((8, 64, COL_DEV), bf16),
            jax.ShapeDtypeStruct((8, 64, HALF), bf16),
            jax.ShapeDtypeStruct((1, HALF), f32),
        ),
        in_specs=[ANY, ANY, ANY, ANY, VMEM, VMEM, VMEM],
        out_specs=[VMEM] * 4,
        scratch_shapes=[
            pltpu.VMEM((16, WIDE), f32),
            pltpu.VMEM((16, WIDE), f32),
            pltpu.VMEM((16, WIDE), f32),
            pltpu.VMEM((16, TILE + 2 * HW), f32),
            pltpu.VMEM((16, TILE), bf16),
            pltpu.VMEM((NB, TABLE), jnp.int32),
            pltpu.VMEM((NB, TABLE), f32),
            pltpu.VMEM((8, 64, HALF), bf16),
            pltpu.VMEM((8, 64, HALF), bf16),
            pltpu.VMEM((8, HALF), f32),
            pltpu.VMEM((8, HALF), f32),
            dma((4,)), dma((6,)), dma((6,)), dma((3,)), dma((3,)), dma((3,)), dma((3,)),
            dma((2,)), dma((2,)), dma((2,)), dma((2,)),
        ],
        compiler_params=pltpu.CompilerParams(
            collective_id=0, has_side_effects=True, vmem_limit_bytes=24 * 2**20),
        name="gather",
    )(potential, species_inputs, diffusion, neighbours, listing, day_count, zenith.reshape(1, COL_DEV))
    lw, sw = radiate(
        cols, work, mu,
        (lw_first, lw_bias, lw_second, lw_depth, lw_fraction),
        (sw_first, sw_bias, sw_second, sw_depth, solar_flux))
    return pl.pallas_call(
        spread_kernel,
        out_shape=jax.ShapeDtypeStruct((16, TILE), f32),
        in_specs=[VMEM] * 5,
        out_specs=VMEM,
        scratch_shapes=[
            pltpu.VMEM((64, HALF), f32),
            pltpu.VMEM((64, COL_DEV), f32),
            pltpu.VMEM((16, TILE), f32),
            dma(()), dma(()), dma((3,)), dma((3,)),
        ],
        compiler_params=pltpu.CompilerParams(
            collective_id=1, has_side_effects=True, vmem_limit_bytes=16 * 2**20),
        name="spread",
    )(lw, sw, base, listing, day_count)


def solution(mesh):
    return jax.shard_map(
        per_device,
        mesh=mesh,
        in_specs=(
            P("group", "tile"), P(None, "group", "tile"), P(None, "tile"), P(None, "tile"),
            P("group", "tile", None), P("group", "tile"), P("group", "tile", None),
            P(), P(), P(), P(), P(), P(), P(), P(), P(), P(),
        ),
        out_specs=P("group", "tile"),
        check_vma=False,
    )
```

```python
import math

import jax
import jax.numpy as jnp
from jax import lax
from jax.experimental import pallas as pl
from jax.experimental.pallas import tpu as pltpu
from jax.sharding import PartitionSpec as P

COL_DEV = 256
HALF = 128
TILE = 1024
NB = 4
HW = 256
GAS = 7
f32, bf16 = jnp.float32, jnp.bfloat16
MESH = pl.DeviceIdType.MESH

LOG2E = 1.4426950408889634
CLAMP = 120.0
N_GROUP = 4
WIDE = TILE + 6 * HW
TABLE = TILE + 4 * HW
LEV = 64
PAIR = 2


def silu(x):
    half = 0.5 * x
    return half + half * jnp.tanh(half)


def soft2(y):
    return jnp.maximum(y, jnp.log2(1.0 + jnp.exp2(jnp.minimum(y, CLAMP))))


def in_two(w):
    high = w.astype(bf16)
    return jnp.concatenate([high, (w - high.astype(f32)).astype(bf16)], axis=1)


def turned(w):
    return jnp.transpose(w.astype(f32))


def spread_first(dst, w_ref):
    col = lax.broadcasted_iota(jnp.int32, (8, 128), 1)
    row = lax.broadcasted_iota(jnp.int32, (8, 128), 0)
    spread = (col // 16 == row).astype(f32).astype(bf16)
    wide = jnp.dot(turned(w_ref[...]).astype(bf16), spread, preferred_element_type=f32)
    lane = jnp.bitwise_and(lax.broadcasted_iota(jnp.int32, (64, 128), 1), 15)
    for l in range(16):
        dst[l * 64 : (l + 1) * 64, :] = jnp.where(lane == l, wide, 0.0).astype(bf16)


def two_blocks(dst, w_ref):
    wt = turned(w_ref[...])
    zero = jnp.zeros((64, 64), f32)
    dst[:64, :] = jnp.concatenate([wt, zero], axis=1).astype(bf16)
    dst[64:, :] = jnp.concatenate([zero, wt], axis=1).astype(bf16)


def down(row, width):
    return jnp.transpose(jnp.broadcast_to(row, (128, width)))


def hidden(h2, x_ref, first, second, bias, width, blk):
    x = x_ref[:, pl.ds(pl.multiple_of(blk * 16, 16), 16), :].reshape(128, width)
    for q in range(8):
        pre = jnp.dot(first[q * 128 : (q + 1) * 128, :], x, preferred_element_type=f32)
        one = silu(pre.reshape(2, 64, width) + bias[None]).reshape(128, width).astype(bf16)
        two = silu(jnp.dot(second[...], one, preferred_element_type=f32))
        h2[q * 128 : (q + 1) * 128, :width] = two.astype(bf16)


def longwave(lo, hi, cols, h2, a1, a2, bias, heads, s_ref, e_ref, lw):
    @pl.loop(lo, hi)
    def _(blk):
        hidden(h2, cols, a1, a2, bias[...], COL_DEV, blk)
        for i in range(16 // PAIR):
            h = jnp.concatenate(
                [h2[(i * PAIR + u) * 64 : (i * PAIR + u + 1) * 64, :] for u in range(PAIR)], axis=1)
            y = jnp.dot(heads[...], jnp.concatenate([h, h], axis=0), preferred_element_type=f32)
            totals = [jnp.zeros((8, COL_DEV), f32) for _ in range(PAIR)]
            for g in range(32):
                rows = slice(g * 8, g * 8 + 8)
                s = s_ref[rows]
                above = e_ref[rows]
                for u in range(PAIR):
                    at = slice(u * COL_DEV, (u + 1) * COL_DEV)
                    s = s + soft2(y[g * 16 : g * 16 + 8, at])
                    frac = soft2(y[g * 16 + 8 : g * 16 + 16, at])
                    below = jnp.exp2(-0.1 * s)
                    totals[u] = totals[u] + frac * (above - below)
                    above = below
                s_ref[rows] = s
                e_ref[rows] = above
            for u in range(PAIR):
                lw[pl.ds(blk * 16 + i * PAIR + u, 1), :] = jnp.sum(totals[u], axis=0, keepdims=True)


def shortwave(work, h2, b1, b2, bias, heads, log_flux, mu, ss_ref, sw):
    slope = jnp.broadcast_to(-0.1 / mu, (8, HALF))
    ss_ref[...] = jnp.broadcast_to(-10.0 * mu, (224, HALF)) * log_flux[...]
    top = jnp.sum(jnp.exp2(log_flux[...]), axis=0, keepdims=True)

    def block(blk, above):
        hidden(h2, work, b1, b2, bias[:, :HALF], HALF, blk)
        for i in range(8):
            r = i * 128
            h = jnp.concatenate([h2[r : r + 64, :HALF], h2[r + 64 : r + 128, :HALF]], axis=1)
            y = jnp.dot(heads[...], jnp.concatenate([h, h], axis=0), preferred_element_type=f32)
            upper = jnp.zeros((8, HALF), f32)
            lower = jnp.zeros((8, HALF), f32)
            for g in range(28):
                rows = slice(g * 8, g * 8 + 8)
                s = ss_ref[rows] + soft2(y[rows, :HALF])
                upper = upper + jnp.exp2(s * slope)
                s = s + soft2(y[rows, HALF:])
                ss_ref[rows] = s
                lower = lower + jnp.exp2(s * slope)
            upper = jnp.sum(upper, axis=0, keepdims=True)
            lower = jnp.sum(lower, axis=0, keepdims=True)
            sw[pl.ds(blk * 16 + i * 2, 1), :] = above - upper
            sw[pl.ds(blk * 16 + i * 2 + 1, 1), :] = upper - lower
            above = lower
        return above

    lax.fori_loop(0, 4, block, top)
    sw[...] = sw[...] * (mu * (12.0 / 224))


def section(src, tables, weights, src_shift, lo, hi, put):
    def step(b, c):
        at = lambda j: pl.ds(pl.multiple_of(j * 128, 128), 128)
        reach = [src[:, at(b - src_shift - 2 + s)] for s in range(5)]
        mid = reach[2]
        home = lax.rem(b + 2, 8) * 128
        total = jnp.zeros_like(mid)
        for k in range(NB):
            rel = jnp.broadcast_to(tables[k : k + 1, at(b - 2)] - home, (8, 128))
            lane = jnp.bitwise_and(rel, 127)
            which = jnp.right_shift(rel, 7)
            near = []
            for h in (0, 8):
                part = taken(reach[0][h : h + 8], lane)
                for s in range(1, 5):
                    part = jnp.where(which == s, taken(reach[s][h : h + 8], lane), part)
                near.append(part)
            near = jnp.concatenate(near, axis=0)
            total = total + weights[k : k + 1, at(b - 2)] * (near - mid)
        put(b, at, mid, total)
        return c

    lax.fori_loop(lo, hi, step, 0, unroll=4)


def taken(rows, lane):
    return jnp.take_along_axis(rows, lane, axis=1, mode="promise_in_bounds")


def slots_of(listing):
    cols = lax.broadcasted_iota(jnp.int32, (COL_DEV, COL_DEV), 0)
    slot = lax.broadcasted_iota(jnp.int32, (COL_DEV, COL_DEV), 1).astype(f32)
    return jnp.sum(jnp.where(listing == cols, slot, 0.0), axis=1, keepdims=True)


def kernel(
    pot, species, diff, nbr, lw1_h, lw2_h, ld_h, lf_h, sw1_h, sw2_h, sd_h,
    listing_ref, count_ref, zen_ref, lb_ref, sb_ref, flux_ref,
    out,
    fe, f1, f2, te, third16, base, tables, weights,
    cols, outgoing, arriving, work, mu_send, mu_arrive,
    lw1, lw2, ld, lf, sw1, sw2, sd,
    a1, a2, b1, b2, heads, sw_heads, lw_bias, sw_bias, log_flux, h2, s_ref, e_ref, ss_ref,
    lw, sw, ret, heat, slab,
    local, w_sem, h_send, h_recv, g_send, g_recv, t_send, t_recv, e_send, e_recv,
    d_send, d_recv, r_send, r_recv, s_send, s_recv,
):
    me, tile = lax.axis_index("group"), lax.axis_index("tile")
    n_tile = lax.axis_size("tile")
    right, left = lax.rem(tile + 1, n_tile), lax.rem(tile + n_tile - 1, n_tile)
    partner = tile + 1 - 2 * lax.rem(tile, 2)
    peers = [lax.rem(me + d, N_GROUP) for d in range(1, N_GROUP)]
    levels_of = lambda g: pl.ds(pl.multiple_of(g * 16, 16), 16)
    columns_of = lambda g: pl.ds(pl.multiple_of(g * COL_DEV, COL_DEV), COL_DEV)
    levels, columns = levels_of(me), columns_of(me)

    def remote(src, dst, send, recv, where):
        return pltpu.make_async_remote_copy(
            src_ref=src, dst_ref=dst, send_sem=send, recv_sem=recv,
            device_id=where, device_id_type=MESH)

    barrier = pltpu.get_barrier_semaphore()
    for p in (left, right):
        pl.semaphore_signal(barrier, inc=1, device_id={"tile": p}, device_id_type=MESH)
    for p in peers:
        pl.semaphore_signal(barrier, inc=1, device_id={"group": p}, device_id_type=MESH)

    own = [
        pltpu.make_async_copy(pot, fe.at[:, 3 * HW : 3 * HW + TILE], local.at[0]),
        pltpu.make_async_copy(diff, weights.at[:, 2 * HW : 2 * HW + TILE], local.at[1]),
        pltpu.make_async_copy(nbr, tables.at[:, 2 * HW : 2 * HW + TILE], local.at[2]),
        pltpu.make_async_copy(
            species.at[:, :, columns], cols.at[1 : GAS + 1, levels, :], local.at[3]),
    ]
    stage = [
        pltpu.make_async_copy(src, dst, w_sem.at[i])
        for i, (src, dst) in enumerate(
            [(lw1_h, lw1), (lw2_h, lw2), (ld_h, ld), (lf_h, lf), (sw1_h, sw1), (sw2_h, sw2), (sd_h, sd)])
    ]
    for c in own + stage:
        c.start()
    pl.semaphore_wait(barrier, N_GROUP + 1)

    halo = [
        remote(pot.at[:, : 3 * HW], fe.at[:, 3 * HW + TILE :], h_send.at[0], h_recv.at[0], {"tile": left}),
        remote(pot.at[:, TILE - 3 * HW :], fe.at[:, : 3 * HW], h_send.at[1], h_recv.at[1], {"tile": right}),
        remote(diff.at[:, : 2 * HW], weights.at[:, 2 * HW + TILE :], h_send.at[2], h_recv.at[2], {"tile": left}),
        remote(diff.at[:, TILE - 2 * HW :], weights.at[:, : 2 * HW], h_send.at[3], h_recv.at[3], {"tile": right}),
        remote(nbr.at[:, : 2 * HW], tables.at[:, 2 * HW + TILE :], h_send.at[4], h_recv.at[4], {"tile": left}),
        remote(nbr.at[:, TILE - 2 * HW :], tables.at[:, : 2 * HW], h_send.at[5], h_recv.at[5], {"tile": right}),
    ]
    gas = [
        remote(species.at[:, :, columns_of(p)], cols.at[1 : GAS + 1, levels, :],
               g_send.at[i], g_recv.at[i], {"group": p})
        for i, p in enumerate(peers)
    ]
    for c in halo + gas:
        c.start()

    for c in stage:
        c.wait()
    spread_first(a1, lw1)
    spread_first(b1, sw1)
    two_blocks(a2, lw2)
    two_blocks(b2, sw2)
    depth, frac = turned(ld[...]) * LOG2E, turned(lf[...]) * LOG2E
    woven = jnp.concatenate([depth.reshape(32, 8, 64), frac.reshape(32, 8, 64)], axis=1)
    heads[...] = in_two(woven.reshape(512, 64))
    sw_heads[...] = in_two(turned(sd[...]) * LOG2E)
    bias = down(lb_ref[...], 64)
    lw_bias[...] = jnp.concatenate([bias, bias], axis=1)
    sw_bias[...] = down(sb_ref[...], 64)
    log_flux[...] = down(jnp.log2(flux_ref[...]), 224)
    s_ref[...] = jnp.zeros_like(s_ref)
    e_ref[...] = jnp.ones_like(e_ref)
    count = count_ref[...].astype(f32)
    slot = slots_of(listing_ref[...])
    place = lax.broadcasted_iota(jnp.int32, (COL_DEV, HALF), 1).astype(f32)
    kept = (slot == place) & (place < count)
    sent = (slot == place + count - HALF) & (place >= COL_DEV - count)
    pick = jnp.concatenate([kept.astype(f32), sent.astype(f32)], axis=1).astype(bf16)
    mu_picked = jnp.dot(
        jnp.broadcast_to(zen_ref[...], (16, COL_DEV)), pick, preferred_element_type=f32)
    mu_send[...] = mu_picked[:8, HALF:]

    for c in own[:3]:
        c.wait()
    for c in halo:
        c.wait()

    def put_first(b, at, mid, total):
        f1[:, at(b)] = mid + total

    def put_second(b, at, mid, total):
        f2[:, at(b)] = 0.75 * fe[:, at(b)] + 0.25 * (mid + total)

    def put_third(b, at, mid, total):
        value = fe[:, at(b)] / 3.0 + (2.0 / 3.0) * (mid + total)
        te[:, at(b - 4)] = value
        third16[:, at(b - 6)] = value.astype(bf16)

    def put_base(b, at, mid, total):
        base[:, at(b - 6)] = mid + total

    section(fe, tables, weights, 0, 2, 18, put_first)
    section(f1, tables, weights, 0, 4, 16, put_second)
    section(f2, tables, weights, 0, 6, 14, put_third)

    warm = [
        remote(third16.at[:, columns_of(p)], cols.at[0, levels, :],
               t_send.at[i], t_recv.at[i], {"group": p})
        for i, p in enumerate(peers)
    ]
    edges = [
        remote(te.at[:, HW : 2 * HW], te.at[:, HW + TILE :], e_send.at[0], e_recv.at[0], {"tile": left}),
        remote(te.at[:, TILE : HW + TILE], te.at[:, :HW], e_send.at[1], e_recv.at[1], {"tile": right}),
    ]
    for c in warm + edges:
        c.start()
    cols[0, levels, :] = third16[:, columns]
    own[3].wait()
    for c in gas + warm:
        c.wait()

    picked = jnp.dot(
        cols[...].reshape((GAS + 1) * LEV, COL_DEV), pick, preferred_element_type=f32)
    outgoing[...] = picked[:, HALF:].astype(bf16).reshape(GAS + 1, LEV, HALF)
    swap = [
        remote(outgoing, arriving, d_send.at[0], d_recv.at[0], {"tile": partner}),
        remote(mu_send, mu_arrive, d_send.at[1], d_recv.at[1], {"tile": partner}),
    ]
    for c in swap:
        c.start()
    work[...] = picked[:, :HALF].astype(bf16).reshape(GAS + 1, LEV, HALF)

    longwave(0, 2, cols, h2, a1, a2, lw_bias, heads, s_ref, e_ref, lw)
    for c in swap:
        c.wait()
    work[...] = work[...] + arriving[...]
    mu = mu_picked[:1, :HALF] + mu_arrive[:1, :]
    shortwave(work, h2, b1, b2, sw_bias, sw_heads, log_flux, mu, ss_ref, sw)
    back = remote(sw, ret, r_send, r_recv, {"tile": partner})
    back.start()
    longwave(2, 4, cols, h2, a1, a2, lw_bias, heads, s_ref, e_ref, lw)

    diag = lax.broadcasted_iota(jnp.int32, (COL_DEV, COL_DEV), 0) == lax.broadcasted_iota(
        jnp.int32, (COL_DEV, COL_DEV), 1)
    slot = jnp.sum(jnp.where(diag, slot, 0.0), axis=0, keepdims=True)
    here = slot < jnp.minimum(count, HALF)
    there = (slot >= HALF) & (slot < count)
    index = jnp.where(there, slot + HALF - count, slot).astype(jnp.int32)
    index = jnp.bitwise_and(index, HALF - 1)
    here, there = here.astype(f32), there.astype(f32)
    back.wait()
    planck = jnp.exp(0.25 * cols[0].astype(f32)) * (-(12.0 / 256) * math.log(2.0))
    for half in range(2):
        part = slice(half * HALF, half * HALF + HALF)
        lane = jnp.broadcast_to(index[:, part], (8, HALF))
        for r in range(0, LEV, 8):
            rows = slice(r, r + 8)
            heat[rows, part] = (
                lw[rows, part] * planck[rows, part]
                + here[:, part] * taken(sw[rows, :], lane)
                + there[:, part] * taken(ret[rows, :], lane)
            )
    sends = [
        remote(heat.at[levels_of(p), :], slab.at[:, columns], s_send.at[i], s_recv.at[i], {"group": p})
        for i, p in enumerate(peers)
    ]
    for c in sends:
        c.start()
    slab[:, columns] = heat[levels, :]
    for c in edges:
        c.wait()
    section(te, tables, weights, 4, 6, 14, put_base)
    for c in sends:
        c.wait()
    out[...] = base[...] + slab[...]


VMEM = pl.BlockSpec(memory_space=pltpu.VMEM)
ANY = pl.BlockSpec(memory_space=pl.ANY)


def per_device(
    potential, species_inputs, diffusion, neighbours, sunlit_column_index, day_count, zenith,
    lw_first, lw_bias, lw_second, lw_depth, lw_fraction,
    sw_first, sw_bias, sw_second, sw_depth, solar_flux,
):
    dma = pltpu.SemaphoreType.DMA
    at32 = lambda *shape: pltpu.VMEM(shape, f32)
    at16 = lambda *shape: pltpu.VMEM(shape, bf16)
    return pl.pallas_call(
        kernel,
        out_shape=jax.ShapeDtypeStruct((16, TILE), f32),
        in_specs=[ANY] * 11 + [VMEM] * 6,
        out_specs=VMEM,
        scratch_shapes=[
            at32(16, WIDE), at32(16, WIDE), at32(16, WIDE), at32(16, TILE + 2 * HW),
            at16(16, TILE), at32(16, TILE),
            pltpu.VMEM((NB, TABLE), jnp.int32), at32(NB, TABLE),
            at16(8, LEV, COL_DEV), at16(8, LEV, HALF), at16(8, LEV, HALF), at16(8, LEV, HALF),
            at32(8, HALF), at32(8, HALF),
            at16(8, 64), at16(64, 64), at16(64, 256), at16(64, 256),
            at16(8, 64), at16(64, 64), at16(64, 224),
            at16(1024, 128), at16(128, 128), at16(1024, 128), at16(128, 128),
            at16(512, 128), at16(224, 128),
            at32(64, COL_DEV), at32(64, HALF), at32(224, HALF),
            at16(1024, COL_DEV), at32(256, COL_DEV), at32(256, COL_DEV), at32(224, HALF),
            at32(LEV, COL_DEV), at32(LEV, HALF), at32(LEV, HALF), at32(LEV, COL_DEV), at32(16, TILE),
            dma((4,)), dma((7,)), dma((6,)), dma((6,)), dma((3,)), dma((3,)), dma((3,)), dma((3,)),
            dma((2,)), dma((2,)), dma((2,)), dma((2,)), dma(()), dma(()), dma((3,)), dma((3,)),
        ],
        compiler_params=pltpu.CompilerParams(
            collective_id=0, has_side_effects=True, vmem_limit_bytes=60 * 2**20),
        name="step",
    )(
        potential, species_inputs, diffusion, neighbours,
        lw_first, lw_second, lw_depth, lw_fraction, sw_first, sw_second, sw_depth,
        sunlit_column_index.reshape(1, COL_DEV), day_count, zenith.reshape(1, COL_DEV),
        lw_bias.reshape(1, 64), sw_bias.reshape(1, 64), solar_flux.reshape(1, 224),
    )


def solution(mesh):
    return jax.shard_map(
        per_device,
        mesh=mesh,
        in_specs=(
            P("group", "tile"), P(None, "group", "tile"), P(None, "tile"), P(None, "tile"),
            P("group", "tile", None), P("group", "tile"), P("group", "tile", None),
            P(), P(), P(), P(), P(), P(), P(), P(), P(), P(),
        ),
        out_specs=P("group", "tile"),
        check_vma=False,
    )
```

```python
import math

import jax
import jax.numpy as jnp
from jax import lax
from jax.experimental import pallas as pl
from jax.experimental.pallas import tpu as pltpu
from jax.sharding import PartitionSpec as P

COL_DEV = 256
HALF = 128
TILE = 1024
NB = 4
HW = 256
GAS = 7
f32, bf16 = jnp.float32, jnp.bfloat16
MESH = pl.DeviceIdType.MESH

LOG2E = 1.4426950408889634
CLAMP = 120.0
N_GROUP = 4
WIDE = TILE + 6 * HW
TABLE = TILE + 4 * HW
LEV = 64
PAIR = 2


def silu(x):
    half = 0.5 * x
    return half + half * jnp.tanh(half)


def soft2(y):
    return jnp.maximum(y, jnp.log2(1.0 + jnp.exp2(jnp.minimum(y, CLAMP))))


def in_two(w):
    high = w.astype(bf16)
    return jnp.concatenate([high, (w - high.astype(f32)).astype(bf16)], axis=1)


def turned(w):
    return jnp.transpose(w.astype(f32))


def spread_first(dst, w_ref):
    col = lax.broadcasted_iota(jnp.int32, (8, 128), 1)
    row = lax.broadcasted_iota(jnp.int32, (8, 128), 0)
    spread = (col // 16 == row).astype(f32).astype(bf16)
    wide = jnp.dot(turned(w_ref[...]).astype(bf16), spread, preferred_element_type=f32)
    lane = jnp.bitwise_and(lax.broadcasted_iota(jnp.int32, (64, 128), 1), 15)
    for l in range(16):
        dst[l * 64 : (l + 1) * 64, :] = jnp.where(lane == l, wide, 0.0).astype(bf16)


def two_blocks(dst, w_ref):
    wt = turned(w_ref[...])
    zero = jnp.zeros((64, 64), f32)
    dst[:64, :] = jnp.concatenate([wt, zero], axis=1).astype(bf16)
    dst[64:, :] = jnp.concatenate([zero, wt], axis=1).astype(bf16)


def down(row, width):
    return jnp.transpose(jnp.broadcast_to(row, (128, width)))


def hidden(h2, x_ref, first, second, bias, width, blk):
    x = x_ref[:, pl.ds(pl.multiple_of(blk * 16, 16), 16), :].reshape(128, width)
    for q in range(8):
        pre = jnp.dot(first[q * 128 : (q + 1) * 128, :], x, preferred_element_type=f32)
        one = silu(pre.reshape(2, 64, width) + bias[None]).reshape(128, width).astype(bf16)
        two = silu(jnp.dot(second[...], one, preferred_element_type=f32))
        h2[q * 128 : (q + 1) * 128, :width] = two.astype(bf16)


def longwave(lo, hi, cols, h2, a1, a2, bias, heads, s_ref, e_ref, lw):
    @pl.loop(lo, hi)
    def _(blk):
        hidden(h2, cols, a1, a2, bias[...], COL_DEV, blk)
        for i in range(16 // PAIR):
            h = jnp.concatenate(
                [h2[(i * PAIR + u) * 64 : (i * PAIR + u + 1) * 64, :] for u in range(PAIR)], axis=1)
            y = jnp.dot(heads[...], jnp.concatenate([h, h], axis=0), preferred_element_type=f32)
            totals = [jnp.zeros((8, COL_DEV), f32) for _ in range(PAIR)]
            for g in range(32):
                rows = slice(g * 8, g * 8 + 8)
                s = s_ref[rows]
                above = e_ref[rows]
                for u in range(PAIR):
                    at = slice(u * COL_DEV, (u + 1) * COL_DEV)
                    s = s + soft2(y[g * 16 : g * 16 + 8, at])
                    frac = soft2(y[g * 16 + 8 : g * 16 + 16, at])
                    below = jnp.exp2(-0.1 * s)
                    totals[u] = totals[u] + frac * (above - below)
                    above = below
                s_ref[rows] = s
                e_ref[rows] = above
            for u in range(PAIR):
                lw[pl.ds(blk * 16 + i * PAIR + u, 1), :] = jnp.sum(totals[u], axis=0, keepdims=True)


def shortwave(work, h2, b1, b2, bias, heads, log_flux, mu, ss_ref, sw):
    slope = jnp.broadcast_to(-0.1 / mu, (8, COL_DEV))
    ss_ref[...] = jnp.broadcast_to(-10.0 * mu, (224, COL_DEV)) * log_flux[...]
    top = jnp.sum(jnp.exp2(log_flux[...]), axis=0, keepdims=True)

    def block(blk, above):
        hidden(h2, work, b1, b2, bias[...], COL_DEV, blk)
        for i in range(16 // PAIR):
            h = jnp.concatenate(
                [h2[(i * PAIR + u) * 64 : (i * PAIR + u + 1) * 64, :] for u in range(PAIR)], axis=1)
            y = jnp.dot(heads[...], jnp.concatenate([h, h], axis=0), preferred_element_type=f32)
            totals = [jnp.zeros((8, COL_DEV), f32) for _ in range(PAIR)]
            for g in range(28):
                rows = slice(g * 8, g * 8 + 8)
                s = ss_ref[rows]
                for u in range(PAIR):
                    s = s + soft2(y[rows, u * COL_DEV : (u + 1) * COL_DEV])
                    totals[u] = totals[u] + jnp.exp2(s * slope)
                ss_ref[rows] = s
            for u in range(PAIR):
                below = jnp.sum(totals[u], axis=0, keepdims=True)
                sw[pl.ds(blk * 16 + i * PAIR + u, 1), :] = above - below
                above = below
        return above

    lax.fori_loop(0, 4, block, top)
    sw[...] = sw[...] * (mu * (12.0 / 224))


def section(src, tables, weights, src_shift, lo, hi, put):
    def step(b, c):
        at = lambda j: pl.ds(pl.multiple_of(j * 128, 128), 128)
        reach = [src[:, at(b - src_shift - 2 + s)] for s in range(5)]
        mid = reach[2]
        home = lax.rem(b + 2, 8) * 128
        total = jnp.zeros_like(mid)
        for k in range(NB):
            rel = jnp.broadcast_to(tables[k : k + 1, at(b - 2)] - home, (8, 128))
            lane = jnp.bitwise_and(rel, 127)
            which = jnp.right_shift(rel, 7)
            near = []
            for h in (0, 8):
                part = taken(reach[0][h : h + 8], lane)
                for s in range(1, 5):
                    part = jnp.where(which == s, taken(reach[s][h : h + 8], lane), part)
                near.append(part)
            near = jnp.concatenate(near, axis=0)
            total = total + weights[k : k + 1, at(b - 2)] * (near - mid)
        put(b, at, mid, total)
        return c

    lax.fori_loop(lo, hi, step, 0, unroll=4)


def taken(rows, lane):
    return jnp.take_along_axis(rows, lane, axis=1, mode="promise_in_bounds")


def slots_of(listing):
    cols = lax.broadcasted_iota(jnp.int32, (COL_DEV, COL_DEV), 0)
    slot = lax.broadcasted_iota(jnp.int32, (COL_DEV, COL_DEV), 1).astype(f32)
    return jnp.sum(jnp.where(listing == cols, slot, 0.0), axis=1, keepdims=True)


def kernel(
    pot, species, diff, nbr, lw1_h, lw2_h, ld_h, lf_h, sw1_h, sw2_h, sd_h,
    listing_ref, count_ref, zen_ref, lb_ref, sb_ref, flux_ref,
    out,
    fe, f1, f2, te, third16, base, tables, weights,
    cols, cols_pair, work, pick, list_pair, zen_own, zen_pair,
    lw1, lw2, ld, lf, sw1, sw2, sd,
    a1, a2, b1, b2, heads, sw_heads, lw_bias, sw_bias, log_flux, h2, s_ref, e_ref, ss_ref,
    lw, sw, heat, slab,
    local, w_sem, h_send, h_recv, g_send, g_recv, t_send, t_recv, e_send, e_recv,
    l_send, l_recv, d_send, d_recv, r_send, r_recv, s_send, s_recv,
):
    me, tile = lax.axis_index("group"), lax.axis_index("tile")
    n_tile = lax.axis_size("tile")
    right, left = lax.rem(tile + 1, n_tile), lax.rem(tile + n_tile - 1, n_tile)
    parity = lax.rem(tile, 2)
    first, last = lax.rem(tile, 32) == 0, (lax.rem(tile, 32) == 31) | (tile == n_tile - 1)
    others = jnp.logical_not(first)
    partner = tile + 1 - 2 * parity
    beyond = lax.rem(tile + n_tile - 1 + 2 * parity, n_tile)
    early = (lax.rem(lax.div(tile, 2), 4) < 2).astype(jnp.int32)
    worker = parity == early
    peers = [lax.rem(me + d, N_GROUP) for d in range(1, N_GROUP)]
    levels_of = lambda g: pl.ds(pl.multiple_of(g * 16, 16), 16)
    columns_of = lambda g: pl.ds(pl.multiple_of(g * COL_DEV, COL_DEV), COL_DEV)
    levels, columns = levels_of(me), columns_of(me)

    def remote(src, dst, send, recv, where):
        return pltpu.make_async_remote_copy(
            src_ref=src, dst_ref=dst, send_sem=send, recv_sem=recv,
            device_id=where, device_id_type=MESH)

    barrier = pltpu.get_barrier_semaphore()

    def greet(where):
        pl.semaphore_signal(barrier, inc=1, device_id=where, device_id_type=MESH)

    greet({"tile": partner})
    for p in peers:
        greet({"group": p})

    @pl.when(jnp.logical_not(first | last))
    def _():
        greet({"tile": beyond})

    zen_own[...] = jnp.broadcast_to(zen_ref[...].astype(f32), (8, COL_DEV))

    own = [
        pltpu.make_async_copy(pot, fe.at[:, 3 * HW : 3 * HW + TILE], local.at[0]),
        pltpu.make_async_copy(diff, weights.at[:, 2 * HW : 2 * HW + TILE], local.at[1]),
        pltpu.make_async_copy(nbr, tables.at[:, 2 * HW : 2 * HW + TILE], local.at[2]),
        pltpu.make_async_copy(
            species.at[:, :, columns], cols.at[1 : GAS + 1, levels, :], local.at[3]),
    ]
    stage = [
        pltpu.make_async_copy(src, dst, w_sem.at[i])
        for i, (src, dst) in enumerate(
            [(lw1_h, lw1), (lw2_h, lw2), (ld_h, ld), (lf_h, lf), (sw1_h, sw1), (sw2_h, sw2), (sd_h, sd)])
    ]
    for c in own + stage:
        c.start()
    pl.semaphore_wait(barrier, N_GROUP + others.astype(jnp.int32))

    @pl.when(first | last)
    def _():
        greet({"tile": beyond})

    to_left = [
        remote(pot.at[:, : 3 * HW], fe.at[:, 3 * HW + TILE :], h_send.at[0], h_recv.at[0], {"tile": left}),
        remote(diff.at[:, : 2 * HW], weights.at[:, 2 * HW + TILE :], h_send.at[1], h_recv.at[1], {"tile": left}),
        remote(nbr.at[:, : 2 * HW], tables.at[:, 2 * HW + TILE :], h_send.at[2], h_recv.at[2], {"tile": left}),
    ]
    to_right = [
        remote(pot.at[:, TILE - 3 * HW :], fe.at[:, : 3 * HW], h_send.at[3], h_recv.at[3], {"tile": right}),
        remote(diff.at[:, TILE - 2 * HW :], weights.at[:, : 2 * HW], h_send.at[4], h_recv.at[4], {"tile": right}),
        remote(nbr.at[:, TILE - 2 * HW :], tables.at[:, : 2 * HW], h_send.at[5], h_recv.at[5], {"tile": right}),
    ]
    gas = [
        remote(species.at[:, :, columns_of(p)], cols.at[1 : GAS + 1, levels, :],
               g_send.at[i], g_recv.at[i], {"group": p})
        for i, p in enumerate(peers)
    ]
    lists = [
        remote(listing_ref, list_pair, l_send.at[0], l_recv.at[0], {"tile": partner}),
        remote(zen_own, zen_pair, l_send.at[1], l_recv.at[1], {"tile": partner}),
    ]

    for c in to_right:
        c.start()

    @pl.when(others)
    def _():
        for c in to_left:
            c.start()

    for c in lists + gas:
        c.start()

    for c in stage:
        c.wait()
    spread_first(a1, lw1)
    spread_first(b1, sw1)
    two_blocks(a2, lw2)
    two_blocks(b2, sw2)
    depth, frac = turned(ld[...]) * LOG2E, turned(lf[...]) * LOG2E
    woven = jnp.concatenate([depth.reshape(32, 8, 64), frac.reshape(32, 8, 64)], axis=1)
    heads[...] = in_two(woven.reshape(512, 64))
    sw_heads[...] = in_two(turned(sd[...]) * LOG2E)
    bias = down(lb_ref[...], 64)
    lw_bias[...] = jnp.concatenate([bias, bias], axis=1)
    bias = down(sb_ref[...], 64)
    sw_bias[...] = jnp.concatenate([bias, bias], axis=1)
    flux = down(jnp.log2(flux_ref[...]), 224)
    log_flux[...] = jnp.concatenate([flux, flux], axis=1)
    s_ref[...] = jnp.zeros_like(s_ref)
    e_ref[...] = jnp.ones_like(e_ref)
    count = count_ref[...].astype(f32)
    slot = slots_of(listing_ref[...])

    @pl.when(first)
    def _():
        pl.semaphore_wait(barrier, 1)
        for c in to_left:
            c.start()

    for c in lists:
        c.wait()
    place = lax.broadcasted_iota(jnp.int32, (COL_DEV, COL_DEV), 1).astype(f32)
    mine = (slot == place) & (place < count)
    theirs = (slots_of(list_pair[...]) == place - count) & (place >= count)
    pick[:COL_DEV, :] = mine.astype(f32).astype(bf16)
    pick[COL_DEV:, :] = theirs.astype(f32).astype(bf16)

    for c in own[:3]:
        c.wait()
    for c in to_left + to_right:
        c.wait()

    def put_first(b, at, mid, total):
        f1[:, at(b)] = mid + total

    def put_second(b, at, mid, total):
        f2[:, at(b)] = 0.75 * fe[:, at(b)] + 0.25 * (mid + total)

    def put_third(b, at, mid, total):
        value = fe[:, at(b)] / 3.0 + (2.0 / 3.0) * (mid + total)
        te[:, at(b - 4)] = value
        third16[:, at(b - 6)] = value.astype(bf16)

    def put_base(b, at, mid, total):
        base[:, at(b - 6)] = mid + total

    section(fe, tables, weights, 0, 2, 18, put_first)
    section(f1, tables, weights, 0, 4, 16, put_second)
    section(f2, tables, weights, 0, 6, 14, put_third)

    warm = [
        remote(third16.at[:, columns_of(p)], cols.at[0, levels, :],
               t_send.at[i], t_recv.at[i], {"group": p})
        for i, p in enumerate(peers)
    ]
    edges = [
        remote(te.at[:, HW : 2 * HW], te.at[:, HW + TILE :], e_send.at[0], e_recv.at[0], {"tile": left}),
        remote(te.at[:, TILE : HW + TILE], te.at[:, :HW], e_send.at[1], e_recv.at[1], {"tile": right}),
    ]
    for c in warm + edges:
        c.start()
    cols[0, levels, :] = third16[:, columns]
    own[3].wait()
    for c in gas + warm:
        c.wait()

    whole = remote(cols, cols_pair, d_send, d_recv, {"tile": partner})
    back = remote(sw, sw, r_send, r_recv, {"tile": partner})

    @pl.when(jnp.logical_not(worker))
    def _():
        whole.start()

    longwave(0, 4, cols, h2, a1, a2, lw_bias, heads, s_ref, e_ref, lw)

    @pl.when(worker)
    def _():
        whole.wait_recv()
        rows = (GAS + 1) * LEV
        both = jnp.dot(cols[...].reshape(rows, COL_DEV), pick[:COL_DEV, :], preferred_element_type=f32)
        both = both + jnp.dot(
            cols_pair[...].reshape(rows, COL_DEV), pick[COL_DEV:, :], preferred_element_type=f32)
        work[...] = both.astype(bf16).reshape(GAS + 1, LEV, COL_DEV)
        mu = jnp.dot(zen_own[...].astype(bf16), pick[:COL_DEV, :], preferred_element_type=f32)
        mu = mu + jnp.dot(zen_pair[...].astype(bf16), pick[COL_DEV:, :], preferred_element_type=f32)
        shortwave(work, h2, b1, b2, sw_bias, sw_heads, log_flux, mu[:1, :], ss_ref, sw)
        back.start()

    for c in edges:
        c.wait()
    section(te, tables, weights, 4, 6, 14, put_base)
    diag = lax.broadcasted_iota(jnp.int32, (COL_DEV, COL_DEV), 0) == lax.broadcasted_iota(
        jnp.int32, (COL_DEV, COL_DEV), 1)
    slot = jnp.sum(jnp.where(diag, slot, 0.0), axis=0, keepdims=True)
    daylit = (slot < count).astype(f32)
    first_slot = jnp.where(worker, 0.0, COL_DEV - count)
    index = jnp.minimum(slot + first_slot, COL_DEV - 1.0).astype(jnp.int32)

    @pl.when(jnp.logical_not(worker))
    def _():
        whole.wait_send()
        back.wait_recv()

    planck = jnp.exp(0.25 * cols[0].astype(f32)) * (-(12.0 / 256) * math.log(2.0))
    for half in range(2):
        part = slice(half * HALF, half * HALF + HALF)
        at = jnp.broadcast_to(index[:, part], (8, HALF))
        lane, upper = jnp.bitwise_and(at, HALF - 1), at >= HALF
        for r in range(0, LEV, 8):
            rows = slice(r, r + 8)
            short = jnp.where(upper, taken(sw[rows, HALF:], lane), taken(sw[rows, :HALF], lane))
            heat[rows, part] = lw[rows, part] * planck[rows, part] + daylit[:, part] * short
    sends = [
        remote(heat.at[levels_of(p), :], slab.at[:, columns], s_send.at[i], s_recv.at[i], {"group": p})
        for i, p in enumerate(peers)
    ]
    for c in sends:
        c.start()
    slab[:, columns] = heat[levels, :]

    @pl.when(worker)
    def _():
        back.wait_send()

    for c in sends:
        c.wait()
    out[...] = base[...] + slab[...]


VMEM = pl.BlockSpec(memory_space=pltpu.VMEM)
ANY = pl.BlockSpec(memory_space=pl.ANY)


def per_device(
    potential, species_inputs, diffusion, neighbours, sunlit_column_index, day_count, zenith,
    lw_first, lw_bias, lw_second, lw_depth, lw_fraction,
    sw_first, sw_bias, sw_second, sw_depth, solar_flux,
):
    dma = pltpu.SemaphoreType.DMA
    at32 = lambda *shape: pltpu.VMEM(shape, f32)
    at16 = lambda *shape: pltpu.VMEM(shape, bf16)
    return pl.pallas_call(
        kernel,
        out_shape=jax.ShapeDtypeStruct((16, TILE), f32),
        in_specs=[ANY] * 11 + [VMEM] * 6,
        out_specs=VMEM,
        scratch_shapes=[
            at32(16, WIDE), at32(16, WIDE), at32(16, WIDE), at32(16, TILE + 2 * HW),
            at16(16, TILE), at32(16, TILE),
            pltpu.VMEM((NB, TABLE), jnp.int32), at32(NB, TABLE),
            at16(8, LEV, COL_DEV), at16(8, LEV, COL_DEV), at16(8, LEV, COL_DEV),
            at16(2 * COL_DEV, COL_DEV), pltpu.VMEM((1, COL_DEV), jnp.int32), at32(8, COL_DEV), at32(8, COL_DEV),
            at16(8, 64), at16(64, 64), at16(64, 256), at16(64, 256),
            at16(8, 64), at16(64, 64), at16(64, 224),
            at16(1024, 128), at16(128, 128), at16(1024, 128), at16(128, 128),
            at16(512, 128), at16(224, 128),
            at32(64, COL_DEV), at32(64, COL_DEV), at32(224, COL_DEV),
            at16(1024, COL_DEV), at32(256, COL_DEV), at32(256, COL_DEV), at32(224, COL_DEV),
            at32(LEV, COL_DEV), at32(LEV, COL_DEV), at32(LEV, COL_DEV), at32(16, TILE),
            dma((4,)), dma((7,)), dma((6,)), dma((6,)), dma((3,)), dma((3,)), dma((3,)), dma((3,)),
            dma((2,)), dma((2,)), dma((2,)), dma((2,)), dma(()), dma(()), dma(()), dma(()), dma((3,)), dma((3,)),
        ],
        compiler_params=pltpu.CompilerParams(
            collective_id=0, has_side_effects=True, vmem_limit_bytes=60 * 2**20),
        name="step",
    )(
        potential, species_inputs, diffusion, neighbours,
        lw_first, lw_second, lw_depth, lw_fraction, sw_first, sw_second, sw_depth,
        sunlit_column_index.reshape(1, COL_DEV), day_count, zenith.reshape(1, COL_DEV),
        lw_bias.reshape(1, 64), sw_bias.reshape(1, 64), solar_flux.reshape(1, 224),
    )


def solution(mesh):
    return jax.shard_map(
        per_device,
        mesh=mesh,
        in_specs=(
            P("group", "tile"), P(None, "group", "tile"), P(None, "tile"), P(None, "tile"),
            P("group", "tile", None), P("group", "tile"), P("group", "tile", None),
            P(), P(), P(), P(), P(), P(), P(), P(), P(), P(),
        ),
        out_specs=P("group", "tile"),
        check_vma=False,
    )
```

```python
import math

import jax
import jax.numpy as jnp
from jax import lax
from jax.experimental import pallas as pl
from jax.experimental.pallas import tpu as pltpu
from jax.sharding import PartitionSpec as P

COL_DEV = 256
HALF = 128
TILE = 1024
NB = 4
HW = 256
GAS = 7
f32, bf16 = jnp.float32, jnp.bfloat16
MESH = pl.DeviceIdType.MESH

LOG2E = 1.4426950408889634
CLAMP = 120.0
N_GROUP = 4
WIDE = TILE + 6 * HW
TABLE = TILE + 4 * HW
LEV = 64
PAIR = 2


def silu(x):
    half = 0.5 * x
    return half + half * jnp.tanh(half)


def soft2(y):
    return jnp.maximum(y, jnp.log2(1.0 + jnp.exp2(jnp.minimum(y, CLAMP))))


def in_two(w):
    high = w.astype(bf16)
    return jnp.concatenate([high, (w - high.astype(f32)).astype(bf16)], axis=1)


def turned(w):
    return jnp.transpose(w.astype(f32))


def spread_first(dst, w_ref):
    col = lax.broadcasted_iota(jnp.int32, (8, 128), 1)
    row = lax.broadcasted_iota(jnp.int32, (8, 128), 0)
    spread = (col // 16 == row).astype(f32).astype(bf16)
    wide = jnp.dot(turned(w_ref[...]).astype(bf16), spread, preferred_element_type=f32)
    lane = jnp.bitwise_and(lax.broadcasted_iota(jnp.int32, (64, 128), 1), 15)
    for l in range(16):
        dst[l * 64 : (l + 1) * 64, :] = jnp.where(lane == l, wide, 0.0).astype(bf16)


def two_blocks(dst, w_ref):
    wt = turned(w_ref[...])
    zero = jnp.zeros((64, 64), f32)
    dst[:64, :] = jnp.concatenate([wt, zero], axis=1).astype(bf16)
    dst[64:, :] = jnp.concatenate([zero, wt], axis=1).astype(bf16)


def down(row, width):
    return jnp.transpose(jnp.broadcast_to(row, (128, width)))


def hidden(h2, x_ref, first, second, bias, width, blk):
    x = x_ref[:, pl.ds(pl.multiple_of(blk * 16, 16), 16), :].reshape(128, width)
    for q in range(8):
        pre = jnp.dot(first[q * 128 : (q + 1) * 128, :], x, preferred_element_type=f32)
        one = silu(pre.reshape(2, 64, width) + bias[None]).reshape(128, width).astype(bf16)
        two = silu(jnp.dot(second[...], one, preferred_element_type=f32))
        h2[q * 128 : (q + 1) * 128, :width] = two.astype(bf16)


def longwave(cols, h2, a1, a2, bias, heads, s_ref, e_ref, lw, hand_on):
    @pl.loop(0, N_GROUP)
    def _(blk):
        hidden(h2, cols, a1, a2, bias[...], COL_DEV, blk)
        for i in range(16 // PAIR):
            h = jnp.concatenate(
                [h2[(i * PAIR + u) * 64 : (i * PAIR + u + 1) * 64, :] for u in range(PAIR)], axis=1)
            y = jnp.dot(heads[...], jnp.concatenate([h, h], axis=0), preferred_element_type=f32)
            totals = [jnp.zeros((8, COL_DEV), f32) for _ in range(PAIR)]
            for g in range(32):
                rows = slice(g * 8, g * 8 + 8)
                s = s_ref[rows]
                above = e_ref[rows]
                for u in range(PAIR):
                    at = slice(u * COL_DEV, (u + 1) * COL_DEV)
                    s = s + soft2(y[g * 16 : g * 16 + 8, at])
                    frac = soft2(y[g * 16 + 8 : g * 16 + 16, at])
                    below = jnp.exp2(-0.1 * s)
                    totals[u] = totals[u] + frac * (above - below)
                    above = below
                s_ref[rows] = s
                e_ref[rows] = above
            for u in range(PAIR):
                lw[i * PAIR + u : i * PAIR + u + 1, :] = jnp.sum(totals[u], axis=0, keepdims=True)
        levels = pl.ds(pl.multiple_of(blk * 16, 16), 16)
        planck = jnp.exp(0.25 * cols[0, levels, :].astype(f32)) * (-(12.0 / 256) * math.log(2.0))
        hand_on(blk, levels, lw[...] * planck)


def shortwave(work, h2, b1, b2, bias, heads, log_flux, mu, ss_ref, sw, hand_on):
    slope = jnp.broadcast_to(-0.1 / mu, (8, COL_DEV))
    ss_ref[...] = jnp.broadcast_to(-10.0 * mu, (224, COL_DEV)) * log_flux[...]
    top = jnp.sum(jnp.exp2(log_flux[...]), axis=0, keepdims=True)

    def block(blk, above):
        hidden(h2, work, b1, b2, bias[...], COL_DEV, blk)
        for i in range(16 // PAIR):
            h = jnp.concatenate(
                [h2[(i * PAIR + u) * 64 : (i * PAIR + u + 1) * 64, :] for u in range(PAIR)], axis=1)
            y = jnp.dot(heads[...], jnp.concatenate([h, h], axis=0), preferred_element_type=f32)
            totals = [jnp.zeros((8, COL_DEV), f32) for _ in range(PAIR)]
            for g in range(28):
                rows = slice(g * 8, g * 8 + 8)
                s = ss_ref[rows]
                for u in range(PAIR):
                    s = s + soft2(y[rows, u * COL_DEV : (u + 1) * COL_DEV])
                    totals[u] = totals[u] + jnp.exp2(s * slope)
                ss_ref[rows] = s
            for u in range(PAIR):
                below = jnp.sum(totals[u], axis=0, keepdims=True)
                sw[i * PAIR + u : i * PAIR + u + 1, :] = above - below
                above = below
        hand_on(blk, pl.ds(pl.multiple_of(blk * 16, 16), 16), sw[...] * (mu * (12.0 / 224)))
        return above

    lax.fori_loop(0, N_GROUP, block, top)


def section(src, tables, weights, src_shift, lo, hi, put):
    def step(b, c):
        at = lambda j: pl.ds(pl.multiple_of(j * 128, 128), 128)
        reach = [src[:, at(b - src_shift - 2 + s)] for s in range(5)]
        mid = reach[2]
        home = lax.rem(b + 2, 8) * 128
        total = jnp.zeros_like(mid)
        for k in range(NB):
            rel = jnp.broadcast_to(tables[k : k + 1, at(b - 2)] - home, (8, 128))
            lane = jnp.bitwise_and(rel, 127)
            which = jnp.right_shift(rel, 7)
            near = []
            for h in (0, 8):
                part = taken(reach[0][h : h + 8], lane)
                for s in range(1, 5):
                    part = jnp.where(which == s, taken(reach[s][h : h + 8], lane), part)
                near.append(part)
            near = jnp.concatenate(near, axis=0)
            total = total + weights[k : k + 1, at(b - 2)] * (near - mid)
        put(b, at, mid, total)
        return c

    lax.fori_loop(lo, hi, step, 0, unroll=hi - lo)


def taken(rows, lane):
    return jnp.take_along_axis(rows, lane, axis=1, mode="promise_in_bounds")


def slots_of(listing):
    cols = lax.broadcasted_iota(jnp.int32, (COL_DEV, COL_DEV), 0)
    slot = lax.broadcasted_iota(jnp.int32, (COL_DEV, COL_DEV), 1).astype(f32)
    return jnp.sum(jnp.where(listing == cols, slot, 0.0), axis=1, keepdims=True)


def kernel(
    pot, species, diff, nbr, lw1_h, lw2_h, ld_h, lf_h, sw1_h, sw2_h, sd_h,
    listing_h, count_h, zen_h, lb_h, sb_h, flux_h,
    out,
    fe, f1, f2, te, third16, base, tables, weights,
    cols, cols_pair, work, pick, list_pair, zen_own, zen_pair,
    lw1, lw2, ld, lf, sw1, sw2, sd, listing_ref, count_ref, zen_ref, lb_ref, sb_ref, flux_ref,
    a1, a2, b1, b2, heads, sw_heads, lw_bias, sw_bias, log_flux, h2, s_ref, e_ref, ss_ref,
    lw, sw, heat, short_own, short_pair, slab, short_slab,
    local, w_sem, h_send, h_recv, g_send, g_recv, t_send, t_recv, e_send, e_recv,
    l_send, l_recv, d_send, d_recv, s_send, s_recv, o_send, o_recv, p_send,
):
    me, tile = lax.axis_index("group"), lax.axis_index("tile")
    n_tile = lax.axis_size("tile")
    right, left = lax.rem(tile + 1, n_tile), lax.rem(tile + n_tile - 1, n_tile)
    parity = lax.rem(tile, 2)
    first, last = lax.rem(tile, 32) == 0, (lax.rem(tile, 32) == 31) | (tile == n_tile - 1)
    others = jnp.logical_not(first)
    partner = tile + 1 - 2 * parity
    beyond = lax.rem(tile + n_tile - 1 + 2 * parity, n_tile)
    early = (lax.rem(lax.div(tile, 2), 4) < 2).astype(jnp.int32)
    worker = parity == early
    peers = [lax.rem(me + d, N_GROUP) for d in range(1, N_GROUP)]
    levels_of = lambda g: pl.ds(pl.multiple_of(g * 16, 16), 16)
    columns_of = lambda g: pl.ds(pl.multiple_of(g * COL_DEV, COL_DEV), COL_DEV)
    levels, columns = levels_of(me), columns_of(me)

    def remote(src, dst, send, recv, where):
        return pltpu.make_async_remote_copy(
            src_ref=src, dst_ref=dst, send_sem=send, recv_sem=recv,
            device_id=where, device_id_type=MESH)

    barrier = pltpu.get_barrier_semaphore()

    def greet(where):
        pl.semaphore_signal(barrier, inc=1, device_id=where, device_id_type=MESH)

    greet({"tile": partner})
    for p in peers:
        greet({"group": p})
        greet({"group": p, "tile": partner})

    @pl.when(jnp.logical_not(first | last))
    def _():
        greet({"tile": beyond})

    own = [
        pltpu.make_async_copy(pot, fe.at[:, 3 * HW : 3 * HW + TILE], local.at[0]),
        pltpu.make_async_copy(diff, weights.at[:, 2 * HW : 2 * HW + TILE], local.at[1]),
        pltpu.make_async_copy(nbr, tables.at[:, 2 * HW : 2 * HW + TILE], local.at[2]),
        pltpu.make_async_copy(
            species.at[:, :, columns], cols.at[1 : GAS + 1, levels, :], local.at[3]),
    ]
    stage = [
        pltpu.make_async_copy(src, dst, w_sem.at[i])
        for i, (src, dst) in enumerate(
            [(lw1_h, lw1), (lw2_h, lw2), (ld_h, ld), (lf_h, lf), (sw1_h, sw1), (sw2_h, sw2), (sd_h, sd),
             (lb_h, lb_ref), (sb_h, sb_ref), (flux_h, flux_ref),
             (listing_h, listing_ref), (count_h, count_ref), (zen_h, zen_ref)])
    ]
    for c in own + stage:
        c.start()
    for c in stage:
        c.wait()
    zen_own[...] = jnp.broadcast_to(zen_ref[...].astype(f32), (8, COL_DEV))
    pl.semaphore_wait(barrier, 2 * N_GROUP - 1 + others.astype(jnp.int32))

    @pl.when(first | last)
    def _():
        greet({"tile": beyond})

    to_left = [
        remote(pot.at[:, : 3 * HW], fe.at[:, 3 * HW + TILE :], h_send.at[0], h_recv.at[0], {"tile": left}),
        remote(diff.at[:, : 2 * HW], weights.at[:, 2 * HW + TILE :], h_send.at[1], h_recv.at[1], {"tile": left}),
        remote(nbr.at[:, : 2 * HW], tables.at[:, 2 * HW + TILE :], h_send.at[2], h_recv.at[2], {"tile": left}),
    ]
    to_right = [
        remote(pot.at[:, TILE - 3 * HW :], fe.at[:, : 3 * HW], h_send.at[3], h_recv.at[3], {"tile": right}),
        remote(diff.at[:, TILE - 2 * HW :], weights.at[:, : 2 * HW], h_send.at[4], h_recv.at[4], {"tile": right}),
        remote(nbr.at[:, TILE - 2 * HW :], tables.at[:, : 2 * HW], h_send.at[5], h_recv.at[5], {"tile": right}),
    ]
    gas = [
        remote(species.at[:, :, columns_of(p)], cols.at[1 : GAS + 1, levels, :],
               g_send.at[i], g_recv.at[i], {"group": p})
        for i, p in enumerate(peers)
    ]
    lists = [
        remote(listing_ref, list_pair, l_send.at[0], l_recv.at[0], {"tile": partner}),
        remote(zen_own, zen_pair, l_send.at[1], l_recv.at[1], {"tile": partner}),
    ]

    for c in to_right:
        c.start()

    @pl.when(others)
    def _():
        for c in to_left:
            c.start()

    for c in lists + gas:
        c.start()

    spread_first(a1, lw1)
    spread_first(b1, sw1)
    two_blocks(a2, lw2)
    two_blocks(b2, sw2)
    depth, frac = turned(ld[...]) * LOG2E, turned(lf[...]) * LOG2E
    woven = jnp.concatenate([depth.reshape(32, 8, 64), frac.reshape(32, 8, 64)], axis=1)
    heads[...] = in_two(woven.reshape(512, 64))
    sw_heads[...] = in_two(turned(sd[...]) * LOG2E)
    bias = down(lb_ref[...], 64)
    lw_bias[...] = jnp.concatenate([bias, bias], axis=1)
    bias = down(sb_ref[...], 64)
    sw_bias[...] = jnp.concatenate([bias, bias], axis=1)
    flux = down(jnp.log2(flux_ref[...]), 224)
    log_flux[...] = jnp.concatenate([flux, flux], axis=1)
    s_ref[...] = jnp.zeros_like(s_ref)
    e_ref[...] = jnp.ones_like(e_ref)
    count = count_ref[...].astype(f32)
    slot = slots_of(listing_ref[...])

    @pl.when(first)
    def _():
        pl.semaphore_wait(barrier, 1)
        for c in to_left:
            c.start()

    for c in lists:
        c.wait()
    pair_slot = slots_of(list_pair[...]) + count
    place = lax.broadcasted_iota(jnp.int32, (COL_DEV, COL_DEV), 1).astype(f32)
    column = lax.broadcasted_iota(jnp.int32, (COL_DEV, COL_DEV), 0).astype(f32)
    pick[:COL_DEV, :] = ((slot == place) & (place < count)).astype(f32).astype(bf16)
    pick[COL_DEV:, :] = ((pair_slot == place) & (place >= count)).astype(f32).astype(bf16)
    across = lambda v: jnp.sum(jnp.where(column == place, v, 0.0), axis=0, keepdims=True)
    slot, pair_slot = across(slot), across(pair_slot)

    for c in own[:3]:
        c.wait()
    for c in to_left + to_right:
        c.wait()

    def put_first(b, at, mid, total):
        f1[:, at(b)] = mid + total

    def put_second(b, at, mid, total):
        f2[:, at(b)] = 0.75 * fe[:, at(b)] + 0.25 * (mid + total)

    def put_third(b, at, mid, total):
        value = fe[:, at(b)] / 3.0 + (2.0 / 3.0) * (mid + total)
        te[:, at(b - 4)] = value
        third16[:, at(b - 6)] = value.astype(bf16)

    def put_base(b, at, mid, total):
        base[:, at(b - 6)] = mid + total

    section(fe, tables, weights, 0, 2, 18, put_first)
    section(f1, tables, weights, 0, 4, 16, put_second)
    section(f2, tables, weights, 0, 6, 14, put_third)

    warm = [
        remote(third16.at[:, columns_of(p)], cols.at[0, levels, :],
               t_send.at[i], t_recv.at[i], {"group": p})
        for i, p in enumerate(peers)
    ]
    edges = [
        remote(te.at[:, HW : 2 * HW], te.at[:, HW + TILE :], e_send.at[0], e_recv.at[0], {"tile": left}),
        remote(te.at[:, TILE : HW + TILE], te.at[:, :HW], e_send.at[1], e_recv.at[1], {"tile": right}),
    ]
    for c in warm + edges:
        c.start()
    cols[0, levels, :] = third16[:, columns]
    own[3].wait()
    for c in gas + warm:
        c.wait()

    whole = remote(cols, cols_pair, d_send, d_recv, {"tile": partner})

    @pl.when(jnp.logical_not(worker))
    def _():
        whole.start()

    def hand_long(blk, rows, value):
        d = lax.rem(blk - me + N_GROUP, N_GROUP)
        heat[rows, :] = value

        @pl.when(d == 0)
        def _():
            slab[:, columns] = value

        @pl.when(d > 0)
        def _():
            remote(heat.at[rows, :], slab.at[:, columns], s_send.at[d], s_recv.at[d], {"group": blk}).start()

    def hand_short(blk, rows, value):
        def placed(at, lit, half):
            part = slice(half * HALF, half * HALF + HALF)
            at = jnp.broadcast_to(at[:, part], (8, HALF))
            lane, upper = jnp.bitwise_and(at, HALF - 1), at >= HALF
            both = [
                jnp.where(upper, taken(value[r : r + 8, HALF:], lane), taken(value[r : r + 8, :HALF], lane))
                for r in (0, 8)
            ]
            return jnp.concatenate(both, axis=0) * lit[:, part]

        limit = lambda v: jnp.minimum(v, COL_DEV - 1.0).astype(jnp.int32)
        own_at, pair_at = limit(slot), limit(pair_slot)
        own_lit, pair_lit = (slot < count).astype(f32), (pair_slot < COL_DEV).astype(f32)
        mine = jnp.concatenate([placed(own_at, own_lit, h) for h in range(2)], axis=1)
        short_own[rows, :] = mine
        short_pair[rows, :] = jnp.concatenate([placed(pair_at, pair_lit, h) for h in range(2)], axis=1)
        d = lax.rem(blk - me + N_GROUP, N_GROUP)

        @pl.when(d == 0)
        def _():
            short_slab[:, columns] = mine

        @pl.when(d > 0)
        def _():
            remote(short_own.at[rows, :], short_slab.at[:, columns], o_send.at[d], o_recv.at[d],
                   {"group": blk}).start()

        remote(short_pair.at[rows, :], short_slab.at[:, columns], p_send.at[d], o_recv.at[d],
               {"group": blk, "tile": partner}).start()

    longwave(cols, h2, a1, a2, lw_bias, heads, s_ref, e_ref, lw, hand_long)

    @pl.when(worker)
    def _():
        whole.wait_recv()
        rows = (GAS + 1) * LEV
        both = jnp.dot(cols[...].reshape(rows, COL_DEV), pick[:COL_DEV, :], preferred_element_type=f32)
        both = both + jnp.dot(
            cols_pair[...].reshape(rows, COL_DEV), pick[COL_DEV:, :], preferred_element_type=f32)
        work[...] = both.astype(bf16).reshape(GAS + 1, LEV, COL_DEV)
        mu = jnp.dot(zen_own[...].astype(bf16), pick[:COL_DEV, :], preferred_element_type=f32)
        mu = mu + jnp.dot(zen_pair[...].astype(bf16), pick[COL_DEV:, :], preferred_element_type=f32)
        shortwave(work, h2, b1, b2, sw_bias, sw_heads, log_flux, mu[:1, :], ss_ref, sw, hand_short)

    for c in edges:
        c.wait()
    section(te, tables, weights, 4, 6, 14, put_base)

    def sent(src, dst, send, recv):
        return remote(src.at[:16, :], dst.at[:, columns], send, recv, {"group": peers[0]})

    for d in range(1, N_GROUP):
        c = sent(heat, slab, s_send.at[d], s_recv.at[d])
        c.wait_send()
        c.wait_recv()
        sent(short_own, short_slab, o_send.at[d], o_recv.at[d]).wait_recv()

    @pl.when(worker)
    def _():
        for d in range(N_GROUP):
            sent(short_pair, short_slab, p_send.at[d], o_recv.at[d]).wait_send()
        for d in range(1, N_GROUP):
            sent(short_own, short_slab, o_send.at[d], o_recv.at[d]).wait_send()

    @pl.when(jnp.logical_not(worker))
    def _():
        whole.wait_send()
        sent(short_own, short_slab, o_send.at[0], o_recv.at[0]).wait_recv()

    out[...] = base[...] + slab[...] + short_slab[...]


VMEM = pl.BlockSpec(memory_space=pltpu.VMEM)
ANY = pl.BlockSpec(memory_space=pl.ANY)


def per_device(
    potential, species_inputs, diffusion, neighbours, sunlit_column_index, day_count, zenith,
    lw_first, lw_bias, lw_second, lw_depth, lw_fraction,
    sw_first, sw_bias, sw_second, sw_depth, solar_flux,
):
    dma = pltpu.SemaphoreType.DMA
    at32 = lambda *shape: pltpu.VMEM(shape, f32)
    at16 = lambda *shape: pltpu.VMEM(shape, bf16)
    return pl.pallas_call(
        kernel,
        out_shape=jax.ShapeDtypeStruct((16, TILE), f32),
        in_specs=[ANY] * 17,
        out_specs=VMEM,
        scratch_shapes=[
            at32(16, WIDE), at32(16, WIDE), at32(16, WIDE), at32(16, TILE + 2 * HW),
            at16(16, TILE), at32(16, TILE),
            pltpu.VMEM((NB, TABLE), jnp.int32), at32(NB, TABLE),
            at16(8, LEV, COL_DEV), at16(8, LEV, COL_DEV), at16(8, LEV, COL_DEV),
            at16(2 * COL_DEV, COL_DEV), pltpu.VMEM((1, COL_DEV), jnp.int32), at32(8, COL_DEV), at32(8, COL_DEV),
            at16(8, 64), at16(64, 64), at16(64, 256), at16(64, 256),
            at16(8, 64), at16(64, 64), at16(64, 224),
            pltpu.VMEM((1, COL_DEV), jnp.int32), pltpu.VMEM((1, 1), jnp.int32), at16(1, COL_DEV),
            at32(1, 64), at32(1, 64), at32(1, 224),
            at16(1024, 128), at16(128, 128), at16(1024, 128), at16(128, 128),
            at16(512, 128), at16(224, 128),
            at32(64, COL_DEV), at32(64, COL_DEV), at32(224, COL_DEV),
            at16(1024, COL_DEV), at32(256, COL_DEV), at32(256, COL_DEV), at32(224, COL_DEV),
            at32(16, COL_DEV), at32(16, COL_DEV), at32(LEV, COL_DEV), at32(LEV, COL_DEV), at32(LEV, COL_DEV),
            at32(16, TILE), at32(16, TILE),
            dma((4,)), dma((13,)), dma((6,)), dma((6,)), dma((3,)), dma((3,)), dma((3,)), dma((3,)),
            dma((2,)), dma((2,)), dma((2,)), dma((2,)), dma(()), dma(()),
            dma((4,)), dma((4,)), dma((4,)), dma((4,)), dma((4,)),
        ],
        compiler_params=pltpu.CompilerParams(
            collective_id=0, has_side_effects=True, vmem_limit_bytes=60 * 2**20),
        name="step",
    )(
        potential, species_inputs, diffusion, neighbours,
        lw_first, lw_second, lw_depth, lw_fraction, sw_first, sw_second, sw_depth,
        sunlit_column_index.reshape(1, COL_DEV), day_count, zenith.reshape(1, COL_DEV),
        lw_bias.reshape(1, 64), sw_bias.reshape(1, 64), solar_flux.reshape(1, 224),
    )


def solution(mesh):
    return jax.shard_map(
        per_device,
        mesh=mesh,
        in_specs=(
            P("group", "tile"), P(None, "group", "tile"), P(None, "tile"), P(None, "tile"),
            P("group", "tile", None), P("group", "tile"), P("group", "tile", None),
            P(), P(), P(), P(), P(), P(), P(), P(), P(), P(),
        ),
        out_specs=P("group", "tile"),
        check_vma=False,
    )
```

```python
import math

import jax
import jax.numpy as jnp
from jax import lax
from jax.experimental import pallas as pl
from jax.experimental.pallas import tpu as pltpu
from jax.sharding import PartitionSpec as P

COL_DEV = 256
HALF = 128
TILE = 1024
NB = 4
HW = 256
GAS = 7
f32, bf16 = jnp.float32, jnp.bfloat16
MESH = pl.DeviceIdType.MESH

LOG2E = 1.4426950408889634
CLAMP = 120.0
N_GROUP = 4
WIDE = TILE + 6 * HW
TABLE = TILE + 4 * HW
LEV = 64
PAIR = 2


def silu(x):
    half = 0.5 * x
    return half + half * jnp.tanh(half)


def soft2(y):
    return jnp.maximum(y, jnp.log2(1.0 + jnp.exp2(jnp.minimum(y, CLAMP))))


def in_two(w):
    high = w.astype(bf16)
    return jnp.concatenate([high, (w - high.astype(f32)).astype(bf16)], axis=1)


def turned(w):
    return jnp.transpose(w.astype(f32))


def spread_first(dst, w_ref):
    col = lax.broadcasted_iota(jnp.int32, (8, 128), 1)
    row = lax.broadcasted_iota(jnp.int32, (8, 128), 0)
    spread = (col // 16 == row).astype(f32).astype(bf16)
    wide = jnp.dot(turned(w_ref[...]).astype(bf16), spread, preferred_element_type=f32)
    lane = jnp.bitwise_and(lax.broadcasted_iota(jnp.int32, (64, 128), 1), 15)
    for l in range(16):
        dst[l * 64 : (l + 1) * 64, :] = jnp.where(lane == l, wide, 0.0).astype(bf16)


def two_blocks(dst, w_ref):
    wt = turned(w_ref[...])
    zero = jnp.zeros((64, 64), f32)
    dst[:64, :] = jnp.concatenate([wt, zero], axis=1).astype(bf16)
    dst[64:, :] = jnp.concatenate([zero, wt], axis=1).astype(bf16)


def down(row, width):
    return jnp.transpose(jnp.broadcast_to(row, (128, width)))


def hidden(h2, x_ref, first, second, bias, width, blk):
    x = x_ref[:, pl.ds(pl.multiple_of(blk * 16, 16), 16), :].reshape(128, width)
    for q in range(8):
        pre = jnp.dot(first[q * 128 : (q + 1) * 128, :], x, preferred_element_type=f32)
        one = silu(pre.reshape(2, 64, width) + bias[None]).reshape(128, width).astype(bf16)
        two = silu(jnp.dot(second[...], one, preferred_element_type=f32))
        h2[q * 128 : (q + 1) * 128, :width] = two.astype(bf16)


def longwave(cols, h2, a1, a2, bias, heads, s_ref, e_ref, lw, arrived, hand_on):
    @pl.loop(0, N_GROUP)
    def _(blk):
        arrived(blk)
        hidden(h2, cols, a1, a2, bias[...], COL_DEV, blk)
        for i in range(16 // PAIR):
            h = jnp.concatenate(
                [h2[(i * PAIR + u) * 64 : (i * PAIR + u + 1) * 64, :] for u in range(PAIR)], axis=1)
            y = jnp.dot(heads[...], jnp.concatenate([h, h], axis=0), preferred_element_type=f32)
            totals = [jnp.zeros((8, COL_DEV), f32) for _ in range(PAIR)]
            for g in range(32):
                rows = slice(g * 8, g * 8 + 8)
                s = s_ref[rows]
                above = e_ref[rows]
                for u in range(PAIR):
                    at = slice(u * COL_DEV, (u + 1) * COL_DEV)
                    s = s + soft2(y[g * 16 : g * 16 + 8, at])
                    frac = soft2(y[g * 16 + 8 : g * 16 + 16, at])
                    below = jnp.exp2(-0.1 * s)
                    totals[u] = totals[u] + frac * (above - below)
                    above = below
                s_ref[rows] = s
                e_ref[rows] = above
            for u in range(PAIR):
                lw[i * PAIR + u : i * PAIR + u + 1, :] = jnp.sum(totals[u], axis=0, keepdims=True)
        levels = pl.ds(pl.multiple_of(blk * 16, 16), 16)
        planck = jnp.exp(0.25 * cols[0, levels, :].astype(f32)) * (-(12.0 / 256) * math.log(2.0))
        hand_on(blk, levels, lw[...] * planck)


def shortwave(work, h2, b1, b2, bias, heads, log_flux, mu, ss_ref, sw, hand_on):
    slope = jnp.broadcast_to(-0.1 / mu, (8, COL_DEV))
    ss_ref[...] = jnp.broadcast_to(-10.0 * mu, (224, COL_DEV)) * log_flux[...]
    top = jnp.sum(jnp.exp2(log_flux[...]), axis=0, keepdims=True)

    def block(blk, above):
        hidden(h2, work, b1, b2, bias[...], COL_DEV, blk)
        for i in range(16 // PAIR):
            h = jnp.concatenate(
                [h2[(i * PAIR + u) * 64 : (i * PAIR + u + 1) * 64, :] for u in range(PAIR)], axis=1)
            y = jnp.dot(heads[...], jnp.concatenate([h, h], axis=0), preferred_element_type=f32)
            totals = [jnp.zeros((8, COL_DEV), f32) for _ in range(PAIR)]
            for g in range(28):
                rows = slice(g * 8, g * 8 + 8)
                s = ss_ref[rows]
                for u in range(PAIR):
                    s = s + soft2(y[rows, u * COL_DEV : (u + 1) * COL_DEV])
                    totals[u] = totals[u] + jnp.exp2(s * slope)
                ss_ref[rows] = s
            for u in range(PAIR):
                below = jnp.sum(totals[u], axis=0, keepdims=True)
                sw[i * PAIR + u : i * PAIR + u + 1, :] = above - below
                above = below
        hand_on(blk, pl.ds(pl.multiple_of(blk * 16, 16), 16), sw[...] * (mu * (12.0 / 224)))
        return above

    lax.fori_loop(0, N_GROUP, block, top)


def section(src, tables, weights, src_shift, lo, hi, put):
    def step(b, c):
        at = lambda j: pl.ds(pl.multiple_of(j * 128, 128), 128)
        reach = [src[:, at(b - src_shift - 2 + s)] for s in range(5)]
        mid = reach[2]
        home = lax.rem(b + 2, 8) * 128
        total = jnp.zeros_like(mid)
        for k in range(NB):
            rel = jnp.broadcast_to(tables[k : k + 1, at(b - 2)] - home, (8, 128))
            lane = jnp.bitwise_and(rel, 127)
            which = jnp.right_shift(rel, 7)
            near = []
            for h in (0, 8):
                part = taken(reach[0][h : h + 8], lane)
                for s in range(1, 5):
                    part = jnp.where(which == s, taken(reach[s][h : h + 8], lane), part)
                near.append(part)
            near = jnp.concatenate(near, axis=0)
            total = total + weights[k : k + 1, at(b - 2)] * (near - mid)
        put(b, at, mid, total)
        return c

    lax.fori_loop(lo, hi, step, 0, unroll=hi - lo)


def taken(rows, lane):
    return jnp.take_along_axis(rows, lane, axis=1, mode="promise_in_bounds")


def slots_of(listing):
    cols = lax.broadcasted_iota(jnp.int32, (COL_DEV, COL_DEV), 0)
    slot = lax.broadcasted_iota(jnp.int32, (COL_DEV, COL_DEV), 1).astype(f32)
    return jnp.sum(jnp.where(listing == cols, slot, 0.0), axis=1, keepdims=True)


def kernel(
    pot, species, diff, nbr, lw1_h, lw2_h, ld_h, lf_h, sw1_h, sw2_h, sd_h,
    listing_h, count_h, zen_h, lb_h, sb_h, flux_h,
    out,
    fe, f1, f2, te, third16, base, tables, weights,
    cols, cols_pair, work, pick, list_pair, zen_own, zen_pair,
    lw1, lw2, ld, lf, sw1, sw2, sd, listing_ref, count_ref, zen_ref, lb_ref, sb_ref, flux_ref,
    a1, a2, b1, b2, heads, sw_heads, lw_bias, sw_bias, log_flux, h2, s_ref, e_ref, ss_ref,
    lw, sw, heat, short_own, short_pair, slab, short_slab,
    local, w_sem, h_send, h_recv, g_send, g_recv, t_send, t_recv, e_send, e_recv,
    l_send, l_recv, d_send, d_recv, s_send, s_recv, o_send, o_recv, p_send,
    x_send, x_recv,
):
    me, tile = lax.axis_index("group"), lax.axis_index("tile")
    n_tile = lax.axis_size("tile")
    right, left = lax.rem(tile + 1, n_tile), lax.rem(tile + n_tile - 1, n_tile)
    parity = lax.rem(tile, 2)
    first, last = lax.rem(tile, 32) == 0, (lax.rem(tile, 32) == 31) | (tile == n_tile - 1)
    others = jnp.logical_not(first)
    partner = tile + 1 - 2 * parity
    beyond = lax.rem(tile + n_tile - 1 + 2 * parity, n_tile)
    early = (lax.rem(lax.div(tile, 2), 4) < 2).astype(jnp.int32)
    worker = parity == early
    peers = [lax.rem(me + d, N_GROUP) for d in range(1, N_GROUP)]
    levels_of = lambda g: pl.ds(pl.multiple_of(g * 16, 16), 16)
    columns_of = lambda g: pl.ds(pl.multiple_of(g * COL_DEV, COL_DEV), COL_DEV)
    levels, columns = levels_of(me), columns_of(me)

    def remote(src, dst, send, recv, where):
        return pltpu.make_async_remote_copy(
            src_ref=src, dst_ref=dst, send_sem=send, recv_sem=recv,
            device_id=where, device_id_type=MESH)

    barrier = pltpu.get_barrier_semaphore()

    def greet(where):
        pl.semaphore_signal(barrier, inc=1, device_id=where, device_id_type=MESH)

    greet({"tile": partner})
    for p in peers:
        greet({"group": p})
        greet({"group": p, "tile": partner})

    @pl.when(jnp.logical_not(first | last))
    def _():
        greet({"tile": beyond})

    own = [
        pltpu.make_async_copy(pot, fe.at[:, 3 * HW : 3 * HW + TILE], local.at[0]),
        pltpu.make_async_copy(diff, weights.at[:, 2 * HW : 2 * HW + TILE], local.at[1]),
        pltpu.make_async_copy(nbr, tables.at[:, 2 * HW : 2 * HW + TILE], local.at[2]),
        pltpu.make_async_copy(
            species.at[:, :, columns], cols.at[1 : GAS + 1, levels, :], local.at[3]),
    ]
    stage = [
        pltpu.make_async_copy(src, dst, w_sem.at[i])
        for i, (src, dst) in enumerate(
            [(lw1_h, lw1), (lw2_h, lw2), (ld_h, ld), (lf_h, lf), (sw1_h, sw1), (sw2_h, sw2), (sd_h, sd),
             (lb_h, lb_ref), (sb_h, sb_ref), (flux_h, flux_ref),
             (listing_h, listing_ref), (count_h, count_ref), (zen_h, zen_ref)])
    ]
    for c in own + stage:
        c.start()
    for c in stage:
        c.wait()
    zen_own[...] = jnp.broadcast_to(zen_ref[...].astype(f32), (8, COL_DEV))
    pl.semaphore_wait(barrier, 2 * N_GROUP - 1 + others.astype(jnp.int32))

    @pl.when(first | last)
    def _():
        greet({"tile": beyond})

    to_left = [
        remote(pot.at[:, : 3 * HW], fe.at[:, 3 * HW + TILE :], h_send.at[0], h_recv.at[0], {"tile": left}),
        remote(diff.at[:, : 2 * HW], weights.at[:, 2 * HW + TILE :], h_send.at[1], h_recv.at[1], {"tile": left}),
        remote(nbr.at[:, : 2 * HW], tables.at[:, 2 * HW + TILE :], h_send.at[2], h_recv.at[2], {"tile": left}),
    ]
    to_right = [
        remote(pot.at[:, TILE - 3 * HW :], fe.at[:, : 3 * HW], h_send.at[3], h_recv.at[3], {"tile": right}),
        remote(diff.at[:, TILE - 2 * HW :], weights.at[:, : 2 * HW], h_send.at[4], h_recv.at[4], {"tile": right}),
        remote(nbr.at[:, TILE - 2 * HW :], tables.at[:, : 2 * HW], h_send.at[5], h_recv.at[5], {"tile": right}),
    ]
    gas = [
        remote(species.at[:, :, columns_of(p)], cols.at[1 : GAS + 1, levels, :],
               g_send.at[i], g_recv.at[i], {"group": p})
        for i, p in enumerate(peers)
    ]
    lists = [
        remote(listing_ref, list_pair, l_send.at[0], l_recv.at[0], {"tile": partner}),
        remote(zen_own, zen_pair, l_send.at[1], l_recv.at[1], {"tile": partner}),
    ]

    for c in to_right:
        c.start()

    @pl.when(others)
    def _():
        for c in to_left:
            c.start()

    for c in lists + gas:
        c.start()

    spread_first(a1, lw1)
    spread_first(b1, sw1)
    two_blocks(a2, lw2)
    two_blocks(b2, sw2)
    depth, frac = turned(ld[...]) * LOG2E, turned(lf[...]) * LOG2E
    woven = jnp.concatenate([depth.reshape(32, 8, 64), frac.reshape(32, 8, 64)], axis=1)
    heads[...] = in_two(woven.reshape(512, 64))
    sw_heads[...] = in_two(turned(sd[...]) * LOG2E)
    bias = down(lb_ref[...], 64)
    lw_bias[...] = jnp.concatenate([bias, bias], axis=1)
    bias = down(sb_ref[...], 64)
    sw_bias[...] = jnp.concatenate([bias, bias], axis=1)
    flux = down(jnp.log2(flux_ref[...]), 224)
    log_flux[...] = jnp.concatenate([flux, flux], axis=1)
    s_ref[...] = jnp.zeros_like(s_ref)
    e_ref[...] = jnp.ones_like(e_ref)
    count = count_ref[...].astype(f32)
    slot = slots_of(listing_ref[...])

    @pl.when(first)
    def _():
        pl.semaphore_wait(barrier, 1)
        for c in to_left:
            c.start()

    for c in lists:
        c.wait()
    pair_slot = slots_of(list_pair[...]) + count
    place = lax.broadcasted_iota(jnp.int32, (COL_DEV, COL_DEV), 1).astype(f32)
    column = lax.broadcasted_iota(jnp.int32, (COL_DEV, COL_DEV), 0).astype(f32)
    pick[:COL_DEV, :] = ((slot == place) & (place < count)).astype(f32).astype(bf16)
    pick[COL_DEV:, :] = ((pair_slot == place) & (place >= count)).astype(f32).astype(bf16)
    across = lambda v: jnp.sum(jnp.where(column == place, v, 0.0), axis=0, keepdims=True)
    slot, pair_slot = across(slot), across(pair_slot)

    for c in own[:3]:
        c.wait()
    for c in to_left + to_right:
        c.wait()

    def put_first(b, at, mid, total):
        f1[:, at(b)] = mid + total

    def put_second(b, at, mid, total):
        f2[:, at(b)] = 0.75 * fe[:, at(b)] + 0.25 * (mid + total)

    def put_third(b, at, mid, total):
        value = fe[:, at(b)] / 3.0 + (2.0 / 3.0) * (mid + total)
        te[:, at(b - 4)] = value
        third16[:, at(b - 6)] = value.astype(bf16)

    def put_base(b, at, mid, total):
        base[:, at(b - 6)] = mid + total

    section(fe, tables, weights, 0, 2, 18, put_first)
    section(f1, tables, weights, 0, 4, 16, put_second)
    section(f2, tables, weights, 0, 6, 14, put_third)

    warm = [
        remote(third16.at[:, columns_of(p)], cols.at[0, levels, :],
               t_send.at[i], t_recv.at[i], {"group": p})
        for i, p in enumerate(peers)
    ]
    edges = [
        remote(te.at[:, HW : 2 * HW], te.at[:, HW + TILE :], e_send.at[0], e_recv.at[0], {"tile": left}),
        remote(te.at[:, TILE : HW + TILE], te.at[:, :HW], e_send.at[1], e_recv.at[1], {"tile": right}),
    ]
    warm_pair = [
        remote(third16.at[:, columns_of(p)], cols_pair.at[0, levels, :],
               x_send.at[i], x_recv.at[i], {"group": p, "tile": partner})
        for i, p in enumerate([me] + peers)
    ]
    for c in warm:
        c.start()

    @pl.when(jnp.logical_not(worker))
    def _():
        for c in warm_pair:
            c.start()

    for c in edges:
        c.start()
    cols[0, levels, :] = third16[:, columns]
    own[3].wait()
    for c in gas:
        c.wait()
    whole = remote(cols.at[1:], cols_pair.at[1:], d_send, d_recv, {"tile": partner})

    @pl.when(jnp.logical_not(worker))
    def _():
        whole.start()

    def arrived(blk):
        d = lax.rem(me - blk + N_GROUP, N_GROUP)

        @pl.when(d > 0)
        def _():
            remote(third16.at[:, columns], cols.at[0, levels, :], t_send.at[d - 1], t_recv.at[d - 1],
                   {"group": peers[0]}).wait_recv()

    def hand_long(blk, rows, value):
        d = lax.rem(blk - me + N_GROUP, N_GROUP)
        heat[rows, :] = value

        @pl.when(d == 0)
        def _():
            slab[:, columns] = value

        @pl.when(d > 0)
        def _():
            remote(heat.at[rows, :], slab.at[:, columns], s_send.at[d], s_recv.at[d], {"group": blk}).start()

    def hand_short(blk, rows, value):
        def placed(at, lit, half):
            part = slice(half * HALF, half * HALF + HALF)
            at = jnp.broadcast_to(at[:, part], (8, HALF))
            lane, upper = jnp.bitwise_and(at, HALF - 1), at >= HALF
            both = [
                jnp.where(upper, taken(value[r : r + 8, HALF:], lane), taken(value[r : r + 8, :HALF], lane))
                for r in (0, 8)
            ]
            return jnp.concatenate(both, axis=0) * lit[:, part]

        limit = lambda v: jnp.minimum(v, COL_DEV - 1.0).astype(jnp.int32)
        own_at, pair_at = limit(slot), limit(pair_slot)
        own_lit, pair_lit = (slot < count).astype(f32), (pair_slot < COL_DEV).astype(f32)
        mine = jnp.concatenate([placed(own_at, own_lit, h) for h in range(2)], axis=1)
        short_own[rows, :] = mine
        short_pair[rows, :] = jnp.concatenate([placed(pair_at, pair_lit, h) for h in range(2)], axis=1)
        d = lax.rem(blk - me + N_GROUP, N_GROUP)

        @pl.when(d == 0)
        def _():
            short_slab[:, columns] = mine

        @pl.when(d > 0)
        def _():
            remote(short_own.at[rows, :], short_slab.at[:, columns], o_send.at[d], o_recv.at[d],
                   {"group": blk}).start()

        remote(short_pair.at[rows, :], short_slab.at[:, columns], p_send.at[d], o_recv.at[d],
               {"group": blk, "tile": partner}).start()

    longwave(cols, h2, a1, a2, lw_bias, heads, s_ref, e_ref, lw, arrived, hand_long)

    @pl.when(worker)
    def _():
        whole.wait_recv()
        for c in warm_pair:
            c.wait_recv()
        rows = (GAS + 1) * LEV
        both = jnp.dot(cols[...].reshape(rows, COL_DEV), pick[:COL_DEV, :], preferred_element_type=f32)
        both = both + jnp.dot(
            cols_pair[...].reshape(rows, COL_DEV), pick[COL_DEV:, :], preferred_element_type=f32)
        work[...] = both.astype(bf16).reshape(GAS + 1, LEV, COL_DEV)
        mu = jnp.dot(zen_own[...].astype(bf16), pick[:COL_DEV, :], preferred_element_type=f32)
        mu = mu + jnp.dot(zen_pair[...].astype(bf16), pick[COL_DEV:, :], preferred_element_type=f32)
        shortwave(work, h2, b1, b2, sw_bias, sw_heads, log_flux, mu[:1, :], ss_ref, sw, hand_short)

    for c in edges:
        c.wait()
    section(te, tables, weights, 4, 6, 14, put_base)
    for c in warm:
        c.wait_send()

    def sent(src, dst, send, recv):
        return remote(src.at[:16, :], dst.at[:, columns], send, recv, {"group": peers[0]})

    for d in range(1, N_GROUP):
        c = sent(heat, slab, s_send.at[d], s_recv.at[d])
        c.wait_send()
        c.wait_recv()
        sent(short_own, short_slab, o_send.at[d], o_recv.at[d]).wait_recv()

    @pl.when(worker)
    def _():
        for d in range(N_GROUP):
            sent(short_pair, short_slab, p_send.at[d], o_recv.at[d]).wait_send()
        for d in range(1, N_GROUP):
            sent(short_own, short_slab, o_send.at[d], o_recv.at[d]).wait_send()

    @pl.when(jnp.logical_not(worker))
    def _():
        whole.wait_send()
        for c in warm_pair:
            c.wait_send()
        sent(short_own, short_slab, o_send.at[0], o_recv.at[0]).wait_recv()

    out[...] = base[...] + slab[...] + short_slab[...]


VMEM = pl.BlockSpec(memory_space=pltpu.VMEM)
ANY = pl.BlockSpec(memory_space=pl.ANY)


def per_device(
    potential, species_inputs, diffusion, neighbours, sunlit_column_index, day_count, zenith,
    lw_first, lw_bias, lw_second, lw_depth, lw_fraction,
    sw_first, sw_bias, sw_second, sw_depth, solar_flux,
):
    dma = pltpu.SemaphoreType.DMA
    at32 = lambda *shape: pltpu.VMEM(shape, f32)
    at16 = lambda *shape: pltpu.VMEM(shape, bf16)
    return pl.pallas_call(
        kernel,
        out_shape=jax.ShapeDtypeStruct((16, TILE), f32),
        in_specs=[ANY] * 17,
        out_specs=VMEM,
        scratch_shapes=[
            at32(16, WIDE), at32(16, WIDE), at32(16, WIDE), at32(16, TILE + 2 * HW),
            at16(16, TILE), at32(16, TILE),
            pltpu.VMEM((NB, TABLE), jnp.int32), at32(NB, TABLE),
            at16(8, LEV, COL_DEV), at16(8, LEV, COL_DEV), at16(8, LEV, COL_DEV),
            at16(2 * COL_DEV, COL_DEV), pltpu.VMEM((1, COL_DEV), jnp.int32), at32(8, COL_DEV), at32(8, COL_DEV),
            at16(8, 64), at16(64, 64), at16(64, 256), at16(64, 256),
            at16(8, 64), at16(64, 64), at16(64, 224),
            pltpu.VMEM((1, COL_DEV), jnp.int32), pltpu.VMEM((1, 1), jnp.int32), at16(1, COL_DEV),
            at32(1, 64), at32(1, 64), at32(1, 224),
            at16(1024, 128), at16(128, 128), at16(1024, 128), at16(128, 128),
            at16(512, 128), at16(224, 128),
            at32(64, COL_DEV), at32(64, COL_DEV), at32(224, COL_DEV),
            at16(1024, COL_DEV), at32(256, COL_DEV), at32(256, COL_DEV), at32(224, COL_DEV),
            at32(16, COL_DEV), at32(16, COL_DEV), at32(LEV, COL_DEV), at32(LEV, COL_DEV), at32(LEV, COL_DEV),
            at32(16, TILE), at32(16, TILE),
            dma((4,)), dma((13,)), dma((6,)), dma((6,)), dma((3,)), dma((3,)), dma((3,)), dma((3,)),
            dma((2,)), dma((2,)), dma((2,)), dma((2,)), dma(()), dma(()),
            dma((4,)), dma((4,)), dma((4,)), dma((4,)), dma((4,)), dma((4,)), dma((4,)),
        ],
        compiler_params=pltpu.CompilerParams(
            collective_id=0, has_side_effects=True, vmem_limit_bytes=60 * 2**20),
        name="step",
    )(
        potential, species_inputs, diffusion, neighbours,
        lw_first, lw_second, lw_depth, lw_fraction, sw_first, sw_second, sw_depth,
        sunlit_column_index.reshape(1, COL_DEV), day_count, zenith.reshape(1, COL_DEV),
        lw_bias.reshape(1, 64), sw_bias.reshape(1, 64), solar_flux.reshape(1, 224),
    )


def solution(mesh):
    return jax.shard_map(
        per_device,
        mesh=mesh,
        in_specs=(
            P("group", "tile"), P(None, "group", "tile"), P(None, "tile"), P(None, "tile"),
            P("group", "tile", None), P("group", "tile"), P("group", "tile", None),
            P(), P(), P(), P(), P(), P(), P(), P(), P(), P(),
        ),
        out_specs=P("group", "tile"),
        check_vma=False,
    )
```

```python
import math

import jax
import jax.numpy as jnp
from jax import lax
from jax.experimental import pallas as pl
from jax.experimental.pallas import tpu as pltpu
from jax.sharding import PartitionSpec as P

COL_DEV = 256
HALF = 128
TILE = 1024
NB = 4
HW = 256
GAS = 7
f32, bf16 = jnp.float32, jnp.bfloat16
MESH = pl.DeviceIdType.MESH

LOG2E = 1.4426950408889634
CLAMP = 120.0
N_GROUP = 4
WIDE = TILE + 6 * HW
TABLE = TILE + 4 * HW
LEV = 64
PAIR = 2


def silu(x):
    half = 0.5 * x
    return half + half * jnp.tanh(half)


def soft2(y):
    return jnp.maximum(y, jnp.log2(1.0 + jnp.exp2(jnp.minimum(y, CLAMP))))


def in_two(w):
    high = w.astype(bf16)
    return jnp.concatenate([high, (w - high.astype(f32)).astype(bf16)], axis=1)


def turned(w):
    return jnp.transpose(w.astype(f32))


def spread_first(dst, w_ref):
    col = lax.broadcasted_iota(jnp.int32, (8, 128), 1)
    row = lax.broadcasted_iota(jnp.int32, (8, 128), 0)
    spread = (col // 16 == row).astype(f32).astype(bf16)
    wide = jnp.dot(turned(w_ref[...]).astype(bf16), spread, preferred_element_type=f32)
    lane = jnp.bitwise_and(lax.broadcasted_iota(jnp.int32, (64, 128), 1), 15)
    for l in range(16):
        dst[l * 64 : (l + 1) * 64, :] = jnp.where(lane == l, wide, 0.0).astype(bf16)


def two_blocks(dst, w_ref):
    wt = turned(w_ref[...])
    zero = jnp.zeros((64, 64), f32)
    dst[:64, :] = jnp.concatenate([wt, zero], axis=1).astype(bf16)
    dst[64:, :] = jnp.concatenate([zero, wt], axis=1).astype(bf16)


def down(row, width):
    return jnp.transpose(jnp.broadcast_to(row, (128, width)))


def hidden(h2, x_ref, first, second, bias, width, blk):
    x = x_ref[:, pl.ds(pl.multiple_of(blk * 16, 16), 16), :].reshape(128, width)
    for q in range(8):
        pre = jnp.dot(first[q * 128 : (q + 1) * 128, :], x, preferred_element_type=f32)
        one = silu(pre.reshape(2, 64, width) + bias[None]).reshape(128, width).astype(bf16)
        two = silu(jnp.dot(second[...], one, preferred_element_type=f32))
        h2[q * 128 : (q + 1) * 128, :width] = two.astype(bf16)


def longwave(cols, h2, a1, a2, bias, heads, s_ref, e_ref, lw, arrived, hand_on):
    @pl.loop(0, N_GROUP)
    def _(blk):
        arrived(blk)
        hidden(h2, cols, a1, a2, bias[...], COL_DEV, blk)
        for i in range(16 // PAIR):
            h = jnp.concatenate(
                [h2[(i * PAIR + u) * 64 : (i * PAIR + u + 1) * 64, :] for u in range(PAIR)], axis=1)
            y = jnp.dot(heads[...], jnp.concatenate([h, h], axis=0), preferred_element_type=f32)
            totals = [jnp.zeros((8, COL_DEV), f32) for _ in range(PAIR)]
            for g in range(32):
                rows = slice(g * 8, g * 8 + 8)
                s = s_ref[rows]
                above = e_ref[rows]
                for u in range(PAIR):
                    at = slice(u * COL_DEV, (u + 1) * COL_DEV)
                    s = s + soft2(y[g * 16 : g * 16 + 8, at])
                    frac = soft2(y[g * 16 + 8 : g * 16 + 16, at])
                    below = jnp.exp2(-0.1 * s)
                    totals[u] = totals[u] + frac * (above - below)
                    above = below
                s_ref[rows] = s
                e_ref[rows] = above
            for u in range(PAIR):
                lw[i * PAIR + u : i * PAIR + u + 1, :] = jnp.sum(totals[u], axis=0, keepdims=True)
        levels = pl.ds(pl.multiple_of(blk * 16, 16), 16)
        planck = jnp.exp(0.25 * cols[0, levels, :].astype(f32)) * (-(12.0 / 256) * math.log(2.0))
        hand_on(blk, levels, lw[...] * planck)


def shortwave(work, h2, b1, b2, bias, heads, log_flux, mu, ss_ref, sw, hand_on):
    slope = jnp.broadcast_to(-0.1 / mu, (8, COL_DEV))
    ss_ref[...] = jnp.broadcast_to(-10.0 * mu, (224, COL_DEV)) * log_flux[...]
    top = jnp.sum(jnp.exp2(log_flux[...]), axis=0, keepdims=True)

    def block(blk, above):
        hidden(h2, work, b1, b2, bias[...], COL_DEV, blk)
        for i in range(16 // PAIR):
            h = jnp.concatenate(
                [h2[(i * PAIR + u) * 64 : (i * PAIR + u + 1) * 64, :] for u in range(PAIR)], axis=1)
            y = jnp.dot(heads[...], jnp.concatenate([h, h], axis=0), preferred_element_type=f32)
            totals = [jnp.zeros((8, COL_DEV), f32) for _ in range(PAIR)]
            for g in range(28):
                rows = slice(g * 8, g * 8 + 8)
                s = ss_ref[rows]
                for u in range(PAIR):
                    s = s + soft2(y[rows, u * COL_DEV : (u + 1) * COL_DEV])
                    totals[u] = totals[u] + jnp.exp2(s * slope)
                ss_ref[rows] = s
            for u in range(PAIR):
                below = jnp.sum(totals[u], axis=0, keepdims=True)
                sw[i * PAIR + u : i * PAIR + u + 1, :] = above - below
                above = below
        hand_on(blk, pl.ds(pl.multiple_of(blk * 16, 16), 16), sw[...] * (mu * (12.0 / 224)))
        return above

    lax.fori_loop(0, N_GROUP, block, top)


def section(src, tables, weights, src_shift, lo, hi, put):
    def step(b, c):
        at = lambda j: pl.ds(pl.multiple_of(j * 128, 128), 128)
        reach = [src[:, at(b - src_shift - 2 + s)] for s in range(5)]
        mid = reach[2]
        home = lax.rem(b + 2, 8) * 128
        total = jnp.zeros_like(mid)
        for k in range(NB):
            rel = jnp.broadcast_to(tables[k : k + 1, at(b - 2)] - home, (8, 128))
            lane = jnp.bitwise_and(rel, 127)
            which = jnp.right_shift(rel, 7)
            near = []
            for h in (0, 8):
                part = taken(reach[0][h : h + 8], lane)
                for s in range(1, 5):
                    part = jnp.where(which == s, taken(reach[s][h : h + 8], lane), part)
                near.append(part)
            near = jnp.concatenate(near, axis=0)
            total = total + weights[k : k + 1, at(b - 2)] * (near - mid)
        put(b, at, mid, total)
        return c

    lax.fori_loop(lo, hi, step, 0, unroll=hi - lo)


def taken(rows, lane):
    return jnp.take_along_axis(rows, lane, axis=1, mode="promise_in_bounds")


def slots_of(listing):
    cols = lax.broadcasted_iota(jnp.int32, (COL_DEV, COL_DEV), 0)
    slot = lax.broadcasted_iota(jnp.int32, (COL_DEV, COL_DEV), 1).astype(f32)
    return jnp.sum(jnp.where(listing == cols, slot, 0.0), axis=1, keepdims=True)


def kernel(
    pot, species, diff, nbr, lw1_h, lw2_h, ld_h, lf_h, sw1_h, sw2_h, sd_h,
    listing_h, count_h, zen_h, lb_h, sb_h, flux_h,
    out,
    fe, f1, f2, te, third16, base, tables, weights,
    cols, cols_pair, work, pick, list_pair, zen_own, zen_pair,
    lw1, lw2, ld, lf, sw1, sw2, sd, listing_ref, count_ref, zen_ref, lb_ref, sb_ref, flux_ref,
    a1, a2, b1, b2, heads, sw_heads, lw_bias, sw_bias, log_flux, h2, s_ref, e_ref, ss_ref,
    lw, sw, heat, short_own, short_pair, slab, short_slab,
    local, w_sem, h_send, h_recv, g_send, g_recv, t_send, t_recv, e_send, e_recv,
    l_send, l_recv, d_send, d_recv, s_send, s_recv, o_send, o_recv, p_send,
    x_send, x_recv,
):
    me, tile = lax.axis_index("group"), lax.axis_index("tile")
    n_tile = lax.axis_size("tile")
    right, left = lax.rem(tile + 1, n_tile), lax.rem(tile + n_tile - 1, n_tile)
    parity = lax.rem(tile, 2)
    first, last = lax.rem(tile, 32) == 0, (lax.rem(tile, 32) == 31) | (tile == n_tile - 1)
    others = jnp.logical_not(first)
    partner = tile + 1 - 2 * parity
    beyond = lax.rem(tile + n_tile - 1 + 2 * parity, n_tile)
    early = (lax.rem(lax.div(tile, 2), 4) < 2).astype(jnp.int32)
    worker = parity == early
    peers = [lax.rem(me + d, N_GROUP) for d in range(1, N_GROUP)]
    levels_of = lambda g: pl.ds(pl.multiple_of(g * 16, 16), 16)
    columns_of = lambda g: pl.ds(pl.multiple_of(g * COL_DEV, COL_DEV), COL_DEV)
    levels, columns = levels_of(me), columns_of(me)

    def remote(src, dst, send, recv, where):
        return pltpu.make_async_remote_copy(
            src_ref=src, dst_ref=dst, send_sem=send, recv_sem=recv,
            device_id=where, device_id_type=MESH)

    barrier = pltpu.get_barrier_semaphore()

    def greet(where):
        pl.semaphore_signal(barrier, inc=1, device_id=where, device_id_type=MESH)

    greet({"tile": partner})
    for p in peers:
        greet({"group": p})
        greet({"group": p, "tile": partner})

    @pl.when(jnp.logical_not(first | last))
    def _():
        greet({"tile": beyond})

    own = [
        pltpu.make_async_copy(pot, fe.at[:, 3 * HW : 3 * HW + TILE], local.at[0]),
        pltpu.make_async_copy(diff, weights.at[:, 2 * HW : 2 * HW + TILE], local.at[1]),
        pltpu.make_async_copy(nbr, tables.at[:, 2 * HW : 2 * HW + TILE], local.at[2]),
        pltpu.make_async_copy(
            species.at[:, :, columns], cols.at[1 : GAS + 1, levels, :], local.at[3]),
    ]
    stage = [
        pltpu.make_async_copy(src, dst, w_sem.at[i])
        for i, (src, dst) in enumerate(
            [(lw1_h, lw1), (lw2_h, lw2), (ld_h, ld), (lf_h, lf), (sw1_h, sw1), (sw2_h, sw2), (sd_h, sd),
             (lb_h, lb_ref), (sb_h, sb_ref), (flux_h, flux_ref),
             (listing_h, listing_ref), (count_h, count_ref), (zen_h, zen_ref)])
    ]
    for c in own + stage:
        c.start()
    for c in stage:
        c.wait()
    zen_own[...] = jnp.broadcast_to(zen_ref[...].astype(f32), (8, COL_DEV))
    pl.semaphore_wait(barrier, 2 * N_GROUP - 1 + others.astype(jnp.int32))

    @pl.when(first | last)
    def _():
        greet({"tile": beyond})

    to_left = [
        remote(pot.at[:, : 3 * HW], fe.at[:, 3 * HW + TILE :], h_send.at[0], h_recv.at[0], {"tile": left}),
        remote(diff.at[:, : 2 * HW], weights.at[:, 2 * HW + TILE :], h_send.at[1], h_recv.at[1], {"tile": left}),
        remote(nbr.at[:, : 2 * HW], tables.at[:, 2 * HW + TILE :], h_send.at[2], h_recv.at[2], {"tile": left}),
    ]
    to_right = [
        remote(pot.at[:, TILE - 3 * HW :], fe.at[:, : 3 * HW], h_send.at[3], h_recv.at[3], {"tile": right}),
        remote(diff.at[:, TILE - 2 * HW :], weights.at[:, : 2 * HW], h_send.at[4], h_recv.at[4], {"tile": right}),
        remote(nbr.at[:, TILE - 2 * HW :], tables.at[:, : 2 * HW], h_send.at[5], h_recv.at[5], {"tile": right}),
    ]
    gas = [
        remote(species.at[:, :, columns_of(p)], cols.at[1 : GAS + 1, levels, :],
               g_send.at[i], g_recv.at[i], {"group": p})
        for i, p in enumerate(peers)
    ]
    lists = [
        remote(listing_ref, list_pair, l_send.at[0], l_recv.at[0], {"tile": partner}),
        remote(zen_own, zen_pair, l_send.at[1], l_recv.at[1], {"tile": partner}),
    ]

    for c in to_right:
        c.start()

    @pl.when(others)
    def _():
        for c in to_left:
            c.start()

    for c in lists + gas:
        c.start()

    spread_first(a1, lw1)
    spread_first(b1, sw1)
    two_blocks(a2, lw2)
    two_blocks(b2, sw2)
    depth, frac = turned(ld[...]) * LOG2E, turned(lf[...]) * LOG2E
    woven = jnp.concatenate([depth.reshape(32, 8, 64), frac.reshape(32, 8, 64)], axis=1)
    heads[...] = in_two(woven.reshape(512, 64))
    sw_heads[...] = in_two(turned(sd[...]) * LOG2E)
    bias = down(lb_ref[...], 64)
    lw_bias[...] = jnp.concatenate([bias, bias], axis=1)
    bias = down(sb_ref[...], 64)
    sw_bias[...] = jnp.concatenate([bias, bias], axis=1)
    flux = down(jnp.log2(flux_ref[...]), 224)
    log_flux[...] = jnp.concatenate([flux, flux], axis=1)
    s_ref[...] = jnp.zeros_like(s_ref)
    e_ref[...] = jnp.ones_like(e_ref)
    count = count_ref[...].astype(f32)
    slot = slots_of(listing_ref[...])

    @pl.when(first)
    def _():
        pl.semaphore_wait(barrier, 1)
        for c in to_left:
            c.start()

    for c in lists:
        c.wait_recv()
    pair_slot = slots_of(list_pair[...]) + count
    place = lax.broadcasted_iota(jnp.int32, (COL_DEV, COL_DEV), 1).astype(f32)
    column = lax.broadcasted_iota(jnp.int32, (COL_DEV, COL_DEV), 0).astype(f32)
    pick[:COL_DEV, :] = ((slot == place) & (place < count)).astype(f32).astype(bf16)
    pick[COL_DEV:, :] = ((pair_slot == place) & (place >= count)).astype(f32).astype(bf16)
    across = lambda v: jnp.sum(jnp.where(column == place, v, 0.0), axis=0, keepdims=True)
    slot, pair_slot = across(slot), across(pair_slot)

    for c in own[:3]:
        c.wait()
    for c in to_left + to_right:
        c.wait_recv()

    def put_first(b, at, mid, total):
        f1[:, at(b)] = mid + total

    def put_second(b, at, mid, total):
        f2[:, at(b)] = 0.75 * fe[:, at(b)] + 0.25 * (mid + total)

    def put_third(b, at, mid, total):
        value = fe[:, at(b)] / 3.0 + (2.0 / 3.0) * (mid + total)
        te[:, at(b - 4)] = value
        third16[:, at(b - 6)] = value.astype(bf16)

    def put_base(b, at, mid, total):
        base[:, at(b - 6)] = mid + total

    section(fe, tables, weights, 0, 2, 18, put_first)
    section(f1, tables, weights, 0, 4, 16, put_second)
    section(f2, tables, weights, 0, 6, 14, put_third)

    warm = [
        remote(third16.at[:, columns_of(p)], cols.at[0, levels, :],
               t_send.at[i], t_recv.at[i], {"group": p})
        for i, p in enumerate(peers)
    ]
    edges = [
        remote(te.at[:, HW : 2 * HW], te.at[:, HW + TILE :], e_send.at[0], e_recv.at[0], {"tile": left}),
        remote(te.at[:, TILE : HW + TILE], te.at[:, :HW], e_send.at[1], e_recv.at[1], {"tile": right}),
    ]
    warm_pair = [
        remote(third16.at[:, columns_of(p)], cols_pair.at[0, levels, :],
               x_send.at[i], x_recv.at[i], {"group": p, "tile": partner})
        for i, p in enumerate([me] + peers)
    ]
    for c in warm:
        c.start()

    @pl.when(jnp.logical_not(worker))
    def _():
        for c in warm_pair:
            c.start()

    for c in edges:
        c.start()
    cols[0, levels, :] = third16[:, columns]
    own[3].wait()
    for c in gas:
        c.wait_recv()
    whole = remote(cols.at[1:], cols_pair.at[1:], d_send, d_recv, {"tile": partner})

    @pl.when(jnp.logical_not(worker))
    def _():
        whole.start()

    def arrived(blk):
        d = lax.rem(me - blk + N_GROUP, N_GROUP)

        @pl.when(d > 0)
        def _():
            remote(third16.at[:, columns], cols.at[0, levels, :], t_send.at[d - 1], t_recv.at[d - 1],
                   {"group": peers[0]}).wait_recv()

    def hand_long(blk, rows, value):
        d = lax.rem(blk - me + N_GROUP, N_GROUP)
        heat[rows, :] = value

        @pl.when(d == 0)
        def _():
            slab[:, columns] = value

        @pl.when(d > 0)
        def _():
            remote(heat.at[rows, :], slab.at[:, columns], s_send.at[d], s_recv.at[d], {"group": blk}).start()

    def hand_short(blk, rows, value):
        def placed(at, lit, half):
            part = slice(half * HALF, half * HALF + HALF)
            at = jnp.broadcast_to(at[:, part], (8, HALF))
            lane, upper = jnp.bitwise_and(at, HALF - 1), at >= HALF
            both = [
                jnp.where(upper, taken(value[r : r + 8, HALF:], lane), taken(value[r : r + 8, :HALF], lane))
                for r in (0, 8)
            ]
            return jnp.concatenate(both, axis=0) * lit[:, part]

        limit = lambda v: jnp.minimum(v, COL_DEV - 1.0).astype(jnp.int32)
        own_at, pair_at = limit(slot), limit(pair_slot)
        own_lit, pair_lit = (slot < count).astype(f32), (pair_slot < COL_DEV).astype(f32)
        mine = jnp.concatenate([placed(own_at, own_lit, h) for h in range(2)], axis=1)
        short_own[rows, :] = mine
        short_pair[rows, :] = jnp.concatenate([placed(pair_at, pair_lit, h) for h in range(2)], axis=1)
        d = lax.rem(blk - me + N_GROUP, N_GROUP)

        @pl.when(d == 0)
        def _():
            short_slab[:, columns] = mine

        @pl.when(d > 0)
        def _():
            remote(short_own.at[rows, :], short_slab.at[:, columns], o_send.at[d], o_recv.at[d],
                   {"group": blk}).start()

        remote(short_pair.at[rows, :], short_slab.at[:, columns], p_send.at[d], o_recv.at[d],
               {"group": blk, "tile": partner}).start()

    longwave(cols, h2, a1, a2, lw_bias, heads, s_ref, e_ref, lw, arrived, hand_long)

    @pl.when(worker)
    def _():
        whole.wait_recv()
        for c in warm_pair:
            c.wait_recv()
        rows = (GAS + 1) * LEV
        both = jnp.dot(cols[...].reshape(rows, COL_DEV), pick[:COL_DEV, :], preferred_element_type=f32)
        both = both + jnp.dot(
            cols_pair[...].reshape(rows, COL_DEV), pick[COL_DEV:, :], preferred_element_type=f32)
        work[...] = both.astype(bf16).reshape(GAS + 1, LEV, COL_DEV)
        mu = jnp.dot(zen_own[...].astype(bf16), pick[:COL_DEV, :], preferred_element_type=f32)
        mu = mu + jnp.dot(zen_pair[...].astype(bf16), pick[COL_DEV:, :], preferred_element_type=f32)
        shortwave(work, h2, b1, b2, sw_bias, sw_heads, log_flux, mu[:1, :], ss_ref, sw, hand_short)

    for c in edges:
        c.wait_recv()
    section(te, tables, weights, 4, 6, 14, put_base)
    for c in to_left + to_right + lists + gas + warm + edges:
        c.wait_send()

    def sent(src, dst, send, recv):
        return remote(src.at[:16, :], dst.at[:, columns], send, recv, {"group": peers[0]})

    for d in range(1, N_GROUP):
        c = sent(heat, slab, s_send.at[d], s_recv.at[d])
        c.wait_send()
        c.wait_recv()
        sent(short_own, short_slab, o_send.at[d], o_recv.at[d]).wait_recv()

    @pl.when(worker)
    def _():
        for d in range(N_GROUP):
            sent(short_pair, short_slab, p_send.at[d], o_recv.at[d]).wait_send()
        for d in range(1, N_GROUP):
            sent(short_own, short_slab, o_send.at[d], o_recv.at[d]).wait_send()

    @pl.when(jnp.logical_not(worker))
    def _():
        whole.wait_send()
        for c in warm_pair:
            c.wait_send()
        sent(short_own, short_slab, o_send.at[0], o_recv.at[0]).wait_recv()

    out[...] = base[...] + slab[...] + short_slab[...]


VMEM = pl.BlockSpec(memory_space=pltpu.VMEM)
ANY = pl.BlockSpec(memory_space=pl.ANY)


def per_device(
    potential, species_inputs, diffusion, neighbours, sunlit_column_index, day_count, zenith,
    lw_first, lw_bias, lw_second, lw_depth, lw_fraction,
    sw_first, sw_bias, sw_second, sw_depth, solar_flux,
):
    dma = pltpu.SemaphoreType.DMA
    at32 = lambda *shape: pltpu.VMEM(shape, f32)
    at16 = lambda *shape: pltpu.VMEM(shape, bf16)
    return pl.pallas_call(
        kernel,
        out_shape=jax.ShapeDtypeStruct((16, TILE), f32),
        in_specs=[ANY] * 17,
        out_specs=VMEM,
        scratch_shapes=[
            at32(16, WIDE), at32(16, WIDE), at32(16, WIDE), at32(16, TILE + 2 * HW),
            at16(16, TILE), at32(16, TILE),
            pltpu.VMEM((NB, TABLE), jnp.int32), at32(NB, TABLE),
            at16(8, LEV, COL_DEV), at16(8, LEV, COL_DEV), at16(8, LEV, COL_DEV),
            at16(2 * COL_DEV, COL_DEV), pltpu.VMEM((1, COL_DEV), jnp.int32), at32(8, COL_DEV), at32(8, COL_DEV),
            at16(8, 64), at16(64, 64), at16(64, 256), at16(64, 256),
            at16(8, 64), at16(64, 64), at16(64, 224),
            pltpu.VMEM((1, COL_DEV), jnp.int32), pltpu.VMEM((1, 1), jnp.int32), at16(1, COL_DEV),
            at32(1, 64), at32(1, 64), at32(1, 224),
            at16(1024, 128), at16(128, 128), at16(1024, 128), at16(128, 128),
            at16(512, 128), at16(224, 128),
            at32(64, COL_DEV), at32(64, COL_DEV), at32(224, COL_DEV),
            at16(1024, COL_DEV), at32(256, COL_DEV), at32(256, COL_DEV), at32(224, COL_DEV),
            at32(16, COL_DEV), at32(16, COL_DEV), at32(LEV, COL_DEV), at32(LEV, COL_DEV), at32(LEV, COL_DEV),
            at32(16, TILE), at32(16, TILE),
            dma((4,)), dma((13,)), dma((6,)), dma((6,)), dma((3,)), dma((3,)), dma((3,)), dma((3,)),
            dma((2,)), dma((2,)), dma((2,)), dma((2,)), dma(()), dma(()),
            dma((4,)), dma((4,)), dma((4,)), dma((4,)), dma((4,)), dma((4,)), dma((4,)),
        ],
        compiler_params=pltpu.CompilerParams(
            collective_id=0, has_side_effects=True, vmem_limit_bytes=60 * 2**20),
        name="step",
    )(
        potential, species_inputs, diffusion, neighbours,
        lw_first, lw_second, lw_depth, lw_fraction, sw_first, sw_second, sw_depth,
        sunlit_column_index.reshape(1, COL_DEV), day_count, zenith.reshape(1, COL_DEV),
        lw_bias.reshape(1, 64), sw_bias.reshape(1, 64), solar_flux.reshape(1, 224),
    )


def solution(mesh):
    return jax.shard_map(
        per_device,
        mesh=mesh,
        in_specs=(
            P("group", "tile"), P(None, "group", "tile"), P(None, "tile"), P(None, "tile"),
            P("group", "tile", None), P("group", "tile"), P("group", "tile", None),
            P(), P(), P(), P(), P(), P(), P(), P(), P(), P(),
        ),
        out_specs=P("group", "tile"),
        check_vma=False,
    )
```
